32 devices in a mesh: dp: 8 (over z, y), tensor: 4 (over x, core).
Axes of the slice: x: 2, y: 2, z: 4, core: 2. Of those that a mesh axis runs over, the one named last changes fastest.
Arguments:
- block_input: bfloat16 [12288, 768], P(('dp', 'tensor')), may hold values from -6 to 6
- passage_lengths: int32 [24, 4], P('dp'), may hold values from 0 to 512, as said below
- qkv_weight: bfloat16 [2, 3, 768, 768], P(None, None, 'dp', 'tensor'), may hold values from -0.21875 to 0.21875
- qv_bias: bfloat16 [2, 2, 768], P(None, None, ('tensor', 'dp')), may hold values from -3 to 3
- out_weight: bfloat16 [2, 768, 768], P(None, 'tensor', 'dp'), may hold values from -1.25 to 1.25
- out_bias: float32 [2, 768], replicated, may hold values from -3 to 3
- first_gain: float32 [2, 768], replicated, may hold values from 0.5 to 1.5
- first_shift: float32 [2, 768], replicated, may hold values from -2 to 2
- up_weight: bfloat16 [2, 768, 3072], P(None, 'dp', 'tensor'), may hold values from -0.21875 to 0.21875
- up_bias: bfloat16 [2, 3072], P(None, ('tensor', 'dp')), may hold values from -3 to 3
- down_weight: bfloat16 [2, 3072, 768], P(None, 'tensor', 'dp'), may hold values from -0.109375 to 0.109375
- down_bias: float32 [2, 768], replicated, may hold values from -3 to 3
- second_gain: float32 [2, 768], replicated, may hold values from 0.5 to 1.5
- second_shift: float32 [2, 768], replicated, may hold values from -2 to 2
- output_grad: float32 [12288, 768], P(('dp', 'tensor')), may hold values from -6 to 6
Outputs:
- block_output: float32 [12288, 768], P(('dp', 'tensor'))
- input_grad: float32 [12288, 768], P(('dp', 'tensor'))
- qkv_weight_grad: float32 [2, 3, 768, 768], P(None, None, 'dp', 'tensor')
- qv_bias_grad: float32 [2, 2, 768], P(None, None, ('tensor', 'dp'))
- out_weight_grad: float32 [2, 768, 768], P(None, 'tensor', 'dp')
- out_bias_grad: float32 [2, 768], replicated
- first_gain_grad: float32 [2, 768], replicated
- first_shift_grad: float32 [2, 768], replicated
- up_weight_grad: float32 [2, 768, 3072], P(None, 'dp', 'tensor')
- up_bias_grad: float32 [2, 3072], P(None, ('tensor', 'dp'))
- down_weight_grad: float32 [2, 3072, 768], P(None, 'tensor', 'dp')
- down_bias_grad: float32 [2, 768], replicated
- second_gain_grad: float32 [2, 768], replicated
- second_shift_grad: float32 [2, 768], replicated
The draws below stay inside these ranges and needn't reach their ends.
Inputs may be any that keep to these rules, and one draw needn't show every extreme that they name: `passage_lengths`: in every packed row the passage lengths sum to at least 1 and at most 512, the slots after the last passage being padding; some row of every draw holds one passage of exactly 512 slots; passages may be empty.
All inputs are finite; a program needn't handle non-finite values.
Results may differ from the reference program's by a relative error of at most 0.04.
Values may be sent and summed in bfloat16 or wider, within the bound.
A program may use at most 192 MiB of HBM per device.

```python
import math
import jax
import jax.numpy as jnp
from jax import lax

H = 12
HD = 64
FF = 3072
D = 768
LAYERS = 2
PACK = 512
SEGS = 4
ROWS = 24
TOKENS = 12288


def draw_passage_lengths(key, part):
    first, second, third = jax.random.split(key, 3)
    padding = jax.random.randint(first, (ROWS, 1), 0, PACK * 3 // 10 + 1)
    filled = PACK - padding
    raw = jax.random.randint(second, (ROWS, SEGS - 1), 0, 1025)
    cuts = jnp.sort(raw * raw // 1024 * filled // 1024, axis=1)
    edges = jnp.concatenate([jnp.zeros((ROWS, 1), jnp.int32), cuts, filled], axis=1)
    lengths = edges[:, 1:] - edges[:, :-1]
    chosen = jax.random.randint(third, (), 0, ROWS)
    single = jnp.where(jnp.arange(SEGS)[None, :] == 0, PACK, 0)
    return jnp.where(jnp.arange(ROWS)[:, None] == chosen, single, lengths).astype(jnp.int32)


def levels(own_key, extent, pieces, low, top_value):
    def one(dim, blocks):
        heights = jax.random.uniform(jax.random.fold_in(jax.random.fold_in(own_key, 6), dim), (blocks,), jnp.float32, low / len(pieces), top_value / len(pieces))
        return jnp.repeat(jnp.exp(heights), extent[dim] // blocks).reshape((-1,) + (1,) * (len(extent) - dim - 1))

    level = one(*pieces[0])
    for cut in pieces[1:]:
        level = level * one(*cut)
    return level


def normal_values(own_key, shape, deviation, most, cuts=(), kind=jnp.bfloat16):
    drawn = deviation * jax.random.normal(own_key, shape, jnp.float32)
    if cuts:
        drawn = drawn * levels(own_key, shape, cuts, -0.22, 0.18)
    return jnp.clip(drawn, -most, most).astype(kind)


def setup_inputs(seed: int = 0) -> dict:
    seeds = jax.random.split(jax.random.key(seed), 16)
    block_input = normal_values(seeds[0], (TOKENS, D), 1.0, 6.0, ((0, 32),))
    passage_lengths = draw_passage_lengths(jax.random.fold_in(seeds[15], 71), 0)
    qkv_weight = normal_values(seeds[2], (LAYERS, 3, D, D), D ** -0.5, 0.21875, ((2, 8), (3, 4)))
    qv_bias = normal_values(seeds[3], (LAYERS, 2, D), 0.5, 3.0, ((2, 32),))
    out_weight = normal_values(seeds[4], (LAYERS, D, D), (D // 32) ** -0.5, 1.25, ((1, 4), (2, 8)))
    out_bias = normal_values(seeds[5], (LAYERS, D), 0.5, 3.0, (), jnp.float32)
    first_gain = jnp.clip(1.0 + 0.1 * jax.random.normal(seeds[6], (LAYERS, D), jnp.float32), 0.5, 1.5)
    first_shift = normal_values(seeds[7], (LAYERS, D), 0.3, 2.0, (), jnp.float32)
    up_weight = normal_values(seeds[8], (LAYERS, D, FF), D ** -0.5, 0.21875, ((1, 8), (2, 4)))
    up_bias = normal_values(seeds[9], (LAYERS, FF), 0.5, 3.0, ((1, 32),))
    down_weight = normal_values(seeds[10], (LAYERS, FF, D), FF ** -0.5, 0.109375, ((1, 4), (2, 8)))
    down_bias = normal_values(seeds[11], (LAYERS, D), 0.5, 3.0, (), jnp.float32)
    second_gain = jnp.clip(1.0 + 0.1 * jax.random.normal(seeds[12], (LAYERS, D), jnp.float32), 0.5, 1.5)
    second_shift = normal_values(seeds[13], (LAYERS, D), 0.3, 2.0, (), jnp.float32)
    output_grad = normal_values(seeds[14], (TOKENS, D), 1.0, 6.0, ((0, 32),), jnp.float32)
    return dict(block_input=block_input, passage_lengths=passage_lengths, qkv_weight=qkv_weight, qv_bias=qv_bias, out_weight=out_weight, out_bias=out_bias, first_gain=first_gain, first_shift=first_shift, up_weight=up_weight, up_bias=up_bias, down_weight=down_weight, down_bias=down_bias, second_gain=second_gain, second_shift=second_shift, output_grad=output_grad)


@jax.custom_vjp
def low(v):
    return lax.optimization_barrier(v.astype(jnp.bfloat16)).astype(jnp.float32)

@jax.custom_vjp
def low_back(v):
    return v

def low_keep(v):
    return (low(v), None)

def low_pass(kept, grad):
    return (grad,)

def back_keep(v):
    return (v, None)

def back_low(kept, grad):
    return (low(grad),)
low.defvjp(low_keep, low_pass)
low_back.defvjp(back_keep, back_low)
highest = lax.Precision.HIGHEST
eps = 1e-05

def normalize(value, gain, shift):
    average = lax.optimization_barrier(jnp.mean(value, axis=-1, keepdims=True))
    centered = value - average
    variance = lax.optimization_barrier(jnp.mean(centered * centered, axis=-1, keepdims=True))
    return centered * lax.rsqrt(variance + eps) * gain + shift

def visible(lengths):
    ends = jnp.cumsum(lengths, axis=1, dtype=jnp.int32)
    places = jnp.arange(PACK, dtype=jnp.int32)
    passage = lax.optimization_barrier(jnp.sum((places[None, :, None] >= ends[:, None, :]).astype(jnp.int32), axis=2, dtype=jnp.int32))
    padding = passage == SEGS
    matching = passage[:, :, None] == passage[:, None, :]
    return jnp.logical_and(jnp.logical_not(padding)[:, None, :], jnp.logical_or(matching, padding[:, :, None]))

def attend(query, key, value, allowed):
    scores = low_back(jnp.einsum('qhd,khd->hqk', query, key, precision=highest)) * HD ** (-0.5)
    scores = jnp.where(allowed[None], scores, -jnp.inf)
    probs = jax.nn.softmax(scores, axis=-1)
    return jnp.einsum('hqk,khd->qhd', low(probs), value, precision=highest)

def attend_row(item):
    return jax.checkpoint(attend)(item[0], item[1], item[2], item[3])

def layer_forward(hidden, allowed, weights):
    qkv_weight, qv_bias, out_weight, out_bias, first_gain, first_shift, up_weight, up_bias, down_weight, down_bias, second_gain, second_shift = weights
    count = hidden.shape[0]
    lowered = low(hidden)
    raw = low_back(jnp.einsum('nd,cde->cne', lowered, qkv_weight, precision=highest))
    query = low(raw[0] + qv_bias[0])
    key = low(raw[1])
    value = low(raw[2] + qv_bias[1])
    shape = (count // PACK, PACK, H, HD)
    context = lax.map(attend_row, (query.reshape(shape), key.reshape(shape), value.reshape(shape), allowed))
    context = low(low_back(context.reshape(count, D)))
    first_sum = hidden + low_back(jnp.dot(context, out_weight, precision=highest)) + out_bias
    middle = normalize(first_sum, first_gain, first_shift)
    upper = low_back(jnp.dot(low(middle), up_weight, precision=highest)) + up_bias
    active = low(jax.nn.gelu(upper, approximate=False))
    second_sum = middle + low_back(jnp.dot(active, down_weight, precision=highest)) + down_bias
    return normalize(second_sum, second_gain, second_shift)

def stack_forward(hidden, allowed, params):
    for layer in range(LAYERS):
        hidden = layer_forward(hidden, allowed, tuple((item[layer] for item in params)))
    return hidden

def reference(block_input, passage_lengths, qkv_weight, qv_bias, out_weight, out_bias, first_gain, first_shift, up_weight, up_bias, down_weight, down_bias, second_gain, second_shift, output_grad):
    weights = tuple((item.astype(jnp.float32) for item in (qkv_weight, qv_bias, out_weight, out_bias, first_gain, first_shift, up_weight, up_bias, down_weight, down_bias, second_gain, second_shift)))
    group = math.gcd(ROWS, max(1, 4096 // PACK))
    blocks = ROWS // group
    inputs = block_input.astype(jnp.float32).reshape(blocks, group * PACK, D)
    cotangents = output_grad.astype(jnp.float32).reshape(blocks, group * PACK, D)
    lengths = passage_lengths.reshape(blocks, group, SEGS)

    def step(totals, item):
        hidden, cotangent, lens = item
        allowed = visible(lens)

        def forward(start, params):
            return stack_forward(start, allowed, params)
        result, pull = jax.vjp(forward, hidden, weights)
        hidden_grad, param_grads = pull(cotangent)
        totals = tuple((total + extra for total, extra in zip(totals, param_grads)))
        return (totals, (result, hidden_grad))
    zeros = tuple((jnp.zeros_like(item) for item in weights))
    totals, (results, grads) = lax.scan(step, zeros, (inputs, cotangents, lengths))
    return (results.reshape(TOKENS, D), grads.reshape(TOKENS, D), totals[0], totals[1], totals[2], totals[3], totals[4], totals[5], totals[6], totals[7], totals[8], totals[9], totals[10], totals[11])
```

```python
import functools

import jax
import jax.numpy as jnp
from jax import lax
from jax.experimental import pallas as pl
from jax.experimental.pallas import tpu as pltpu
from jax.sharding import PartitionSpec as P

HD = 64
PACK = 512
BLK = 128
WIN = 2 * PACK
EPS = 1e-05
NEG = -1e30
MESH = pl.DeviceIdType.MESH
BF = jnp.bfloat16
F32 = jnp.float32


def dot(a, b):
    return jnp.dot(a, b, preferred_element_type=F32)


def dot_nt(a, b):
    return lax.dot_general(a, b, (((1,), (1,)), ((), ())), preferred_element_type=F32)


def dot_tn(a, b):
    return lax.dot_general(a, b, (((0,), (0,)), ((), ())), preferred_element_type=F32)


def params(**kw):
    return pltpu.CompilerParams(vmem_limit_bytes=60 * 1024 * 1024, **kw)


def whole(shape):
    return pl.BlockSpec(shape, lambda t: (0,) * len(shape))


def per_t(shape, *rest):
    tail = rest if rest else (0,) * (len(shape) - 1)
    return pl.BlockSpec(shape, lambda t: (t,) + tail)


class Place:
    def __init__(self, n_dp):
        self.nz = n_dp // 2
        dp, tensor = lax.axis_index("dp"), lax.axis_index("tensor")
        self.dp, self.tensor = dp, tensor
        self.z, self.y = dp // 2, dp % 2
        self.x, self.c = tensor // 2, tensor % 2
        self.dp_y = 2 * self.z + 1 - self.y
        self.t_x = 2 * (1 - self.x) + self.c
        self.t_c = 2 * self.x + 1 - self.c
        self.t_xc = 2 * (1 - self.x) + 1 - self.c
        self.to_x = (dp, self.t_x)
        self.to_y = (self.dp_y, tensor)
        self.to_c = (dp, self.t_c)

    def d(self, z, same_y=True):
        return 2 * z + (self.y if same_y else 1 - self.y)


def greet(devices):
    barrier = pltpu.get_barrier_semaphore()
    for device in devices:
        pl.semaphore_signal(barrier, inc=1, device_id=device, device_id_type=MESH)
    pl.semaphore_wait(barrier, len(devices))


def gather_kernel(n_dp, own_ref, out_ref, own_sem, send_sem, recv_sem):
    me = Place(n_dp)
    nz = me.nz
    half = own_ref.shape[1] // 2
    barrier = pltpu.get_barrier_semaphore()
    for device in (me.to_x, me.to_y, me.to_c):
        pl.semaphore_signal(barrier, inc=1, device_id=device, device_id_type=MESH)

    @pl.when(me.z > 0)
    def _():
        pl.semaphore_signal(barrier, inc=1, device_id=(me.dp - 2, me.tensor), device_id_type=MESH)

    @pl.when(me.z < nz - 1)
    def _():
        pl.semaphore_signal(barrier, inc=1, device_id=(me.dp + 2, me.tensor), device_id_type=MESH)

    pl.semaphore_wait(barrier, 3 + (me.z > 0).astype(jnp.int32) + (me.z < nz - 1).astype(jnp.int32))

    def piece(t, d, part):
        if part is None:
            return out_ref.at[t, d]
        return out_ref.at[t, d, :, pl.ds(part * half, half)]

    def copy(source, t, d, part, route, z, device):
        slot = route * nz + z
        return pltpu.make_async_remote_copy(
            src_ref=source if source is not None else piece(t, d, part),
            dst_ref=piece(t, d, part),
            send_sem=send_sem.at[slot],
            recv_sem=recv_sem.at[slot],
            device_id=device,
            device_id_type=MESH,
        )

    mine = pltpu.make_async_copy(own_ref, out_ref.at[me.tensor, me.dp], own_sem)
    mine.start()

    def z_copy(p, up, source=None):
        return copy(source, me.tensor, me.d(p), None, 0, p, (me.dp + 2 if up else me.dp - 2, me.tensor))

    def x_copy(p, source=None):
        return copy(source, me.tensor, me.d(p), None, 1, p, me.to_x)

    def y_copy(p, source=None):
        return copy(source, me.tensor, me.d(p), None, 2, p, me.to_y)

    def first_copy(p):
        return copy(None, me.t_x, me.d(p), 0, 3, p, me.to_y)

    def second_copy(p):
        return copy(None, me.tensor, me.d(p, False), 1, 4, p, me.to_x)

    def core_copy(kind, p, source=None):
        t = me.tensor if kind in (0, 2) else me.t_x
        d = me.d(p, kind in (0, 1))
        part = {3: 0, 4: 1}.get(kind)
        return copy(source, t, d, part, 5 + kind, p, me.to_c)

    def arrived(t, d, part, slot):
        pltpu.make_async_copy(piece(t, d, part), piece(t, d, part), recv_sem.at[slot]).wait()

    def own_round():
        @pl.when(me.z < nz - 1)
        def _():
            z_copy(me.z, True, own_ref).start()

        @pl.when(me.z > 0)
        def _():
            copy(own_ref, me.tensor, me.dp, None, 10, me.z, (me.dp - 2, me.tensor)).start()

        x_copy(me.z, own_ref).start()
        y_copy(me.z, own_ref).start()
        core_copy(0, me.z, own_ref).start()

    def z_round(p, up, valid):
        @pl.when(valid)
        def _():
            arrived(me.tensor, me.d(p), None, (0 if up else 10) * nz + p)

            @pl.when(me.z < nz - 1 if up else me.z > 0)
            def _():
                if up:
                    z_copy(p, True).start()
                else:
                    copy(None, me.tensor, me.d(p), None, 10, p, (me.dp - 2, me.tensor)).start()

            x_copy(p).start()
            y_copy(p).start()
            core_copy(0, p).start()

    def xy_round(p, valid):
        @pl.when(valid)
        def _():
            arrived(me.t_x, me.d(p), None, nz + p)
            first_copy(p).start()
            core_copy(1, p).start()
            arrived(me.tensor, me.d(p, False), None, 2 * nz + p)
            second_copy(p).start()
            core_copy(2, p).start()

    def diagonal_round(p, valid):
        @pl.when(valid)
        def _():
            arrived(me.t_x, me.d(p, False), 0, 3 * nz + p)
            core_copy(3, p).start()
            arrived(me.t_x, me.d(p, False), 1, 4 * nz + p)
            core_copy(4, p).start()

    true = me.z >= 0
    own_round()
    for s in range(1, nz + 2):
        if s < nz:
            z_round(me.z - s, True, me.z - s >= 0)
            z_round(me.z + s, False, me.z + s < nz)
        if s == 1:
            xy_round(me.z, true)
        elif s - 1 < nz:
            xy_round(me.z - s + 1, me.z - s + 1 >= 0)
            xy_round(me.z + s - 1, me.z + s - 1 < nz)
        if s == 2:
            diagonal_round(me.z, true)
        elif 2 < s < nz + 2:
            diagonal_round(me.z - s + 2, me.z - s + 2 >= 0)
            diagonal_round(me.z + s - 2, me.z + s - 2 < nz)

    for p in range(nz):
        for kind in range(5):
            t = me.t_c if kind in (0, 2) else me.t_xc
            part = {3: 0, 4: 1}.get(kind)
            arrived(t, me.d(p, kind in (0, 1)), part, (5 + kind) * nz + p)

    mine.wait()
    for p in range(nz):
        @pl.when(jnp.logical_and(me.z < nz - 1, p <= me.z))
        def _():
            z_copy(p, True).wait_send()

        @pl.when(jnp.logical_and(me.z > 0, p >= me.z))
        def _():
            copy(None, me.tensor, me.d(p), None, 10, p, (me.dp - 2, me.tensor)).wait_send()

        x_copy(p).wait_send()
        y_copy(p).wait_send()
        first_copy(p).wait_send()
        second_copy(p).wait_send()
        for kind in range(5):
            core_copy(kind, p).wait_send()


def gather_weights(own, n_dp, n_tensor, collective_id):
    rows, cols = own.shape
    slots = 11 * (n_dp // 2)
    out = pl.pallas_call(
        functools.partial(gather_kernel, n_dp),
        out_shape=jax.ShapeDtypeStruct((n_tensor, n_dp, rows, cols), own.dtype),
        in_specs=[pl.BlockSpec(memory_space=pltpu.MemorySpace.HBM)],
        out_specs=pl.BlockSpec(memory_space=pltpu.MemorySpace.HBM),
        scratch_shapes=[
            pltpu.SemaphoreType.DMA,
            pltpu.SemaphoreType.DMA((slots,)),
            pltpu.SemaphoreType.DMA((slots,)),
        ],
        compiler_params=pltpu.CompilerParams(collective_id=collective_id, has_side_effects=True),
        name="gather_weights",
    )(own)
    return out.reshape(n_tensor, n_dp * rows, cols)


def scatter_kernel(
    n_dp, g_ref, out_ref, mine, core_in, first_in, second_in, x_in, y_in, z_in, load_sem, send_sem, recv_sem
):
    me = Place(n_dp)
    nz = me.nz
    cols = g_ref.shape[-1]
    half = cols // 2
    zs = [lax.rem(me.z + k, nz) for k in range(1, nz)] + [me.z]
    peers = [me.to_x, me.to_y, me.to_c] + [(me.d(z), me.tensor) for z in zs[:-1]]
    greet(peers)

    def owner(place, k):
        x_other, y_other = place in (0, 1), place in (0, 2)
        return x_other, me.d(zs[k], not y_other)

    def remote(source, target, slot, device):
        return pltpu.make_async_remote_copy(
            src_ref=source, dst_ref=target, send_sem=send_sem.at[slot], recv_sem=recv_sem.at[slot],
            device_id=device, device_id_type=MESH,
        )

    def to_core(place, k):
        x_other, d = owner(place, k)
        return remote(g_ref.at[me.t_xc if x_other else me.t_c, d], core_in.at[place, k], place * nz + k, me.to_c)

    def load(place, k):
        x_other, d = owner(place, k)
        return pltpu.make_async_copy(
            g_ref.at[me.t_x if x_other else me.tensor, d], mine.at[place, k], load_sem.at[place * nz + k]
        )

    for k in range(nz):
        for place in range(4):
            to_core(place, k).start()
            load(place, k).start()

    def first(k):
        return remote(mine.at[0, k, :, pl.ds(0, half)], first_in.at[k], 4 * nz + k, me.to_x)

    def second(k):
        return remote(mine.at[0, k, :, pl.ds(half, half)], second_in.at[k], 5 * nz + k, me.to_y)

    def along_x(k):
        return remote(mine.at[1, k], x_in.at[k], 6 * nz + k, me.to_x)

    def along_y(k):
        return remote(mine.at[2, k], y_in.at[k], 7 * nz + k, me.to_y)

    def along_z(k):
        return remote(mine.at[3, k], z_in.at[k], 8 * nz + k, (me.d(zs[k]), me.tensor))

    def both(place, k):
        load(place, k).wait()
        to_core(place, k).wait_recv()
        return mine[place, k].astype(F32) + core_in[place, k].astype(F32)

    for step in range(nz + 2):
        if step < nz:
            k = step
            mine[0, k] = both(0, k).astype(BF)
            first(k).start()
            second(k).start()
        if 0 <= step - 1 < nz:
            k = step - 1
            total = both(1, k)
            second(k).wait_recv()
            mine[1, k, :, :half] = total[:, :half].astype(BF)
            mine[1, k, :, half:] = (total[:, half:] + second_in[k].astype(F32)).astype(BF)
            along_x(k).start()
            total = both(2, k)
            first(k).wait_recv()
            mine[2, k, :, half:] = total[:, half:].astype(BF)
            mine[2, k, :, :half] = (total[:, :half] + first_in[k].astype(F32)).astype(BF)
            along_y(k).start()
        if 0 <= step - 2 < nz:
            k = step - 2
            total = both(3, k)
            along_x(k).wait_recv()
            total += x_in[k].astype(F32)
            along_y(k).wait_recv()
            total += y_in[k].astype(F32)
            if k < nz - 1:
                mine[3, k] = total.astype(BF)
                along_z(k).start()
            else:
                for j in range(nz - 1):
                    along_z(j).wait_recv()
                    total += z_in[j].astype(F32)
                out_ref[...] = total
    for k in range(nz):
        for place in range(4):
            to_core(place, k).wait_send()
        for made in (first, second, along_x, along_y):
            made(k).wait_send()
        if k < nz - 1:
            along_z(k).wait_send()


def scatter_grads(grads, n_dp, n_tensor, collective_id):
    cols = grads.shape[-1]
    rows = grads.shape[1] // n_dp
    nz = n_dp // 2
    return pl.pallas_call(
        functools.partial(scatter_kernel, n_dp),
        out_shape=jax.ShapeDtypeStruct((rows, cols), F32),
        in_specs=[pl.BlockSpec(memory_space=pltpu.MemorySpace.HBM)],
        out_specs=pl.BlockSpec(memory_space=pltpu.MemorySpace.VMEM),
        scratch_shapes=[
            pltpu.VMEM((4, nz, rows, cols), BF),
            pltpu.VMEM((4, nz, rows, cols), BF),
            pltpu.VMEM((nz, rows, cols // 2), BF),
            pltpu.VMEM((nz, rows, cols // 2), BF),
            pltpu.VMEM((nz, rows, cols), BF),
            pltpu.VMEM((nz, rows, cols), BF),
            pltpu.VMEM((nz - 1, rows, cols), BF),
            pltpu.SemaphoreType.DMA((4 * nz,)),
            pltpu.SemaphoreType.DMA((9 * nz,)),
            pltpu.SemaphoreType.DMA((9 * nz,)),
        ],
        compiler_params=params(collective_id=collective_id, has_side_effects=True),
        name="scatter_grads",
    )(grads.reshape(n_tensor, n_dp, rows, cols))


def window_slots(tokens, rows):
    t = lax.axis_index("tensor")
    count = tokens // BLK
    first = jnp.minimum(t * count * BLK // PACK, rows - 2)
    return [(t * count + j) * BLK // PACK - first for j in range(count)]


def lane_masks(first, count):
    slot = lax.broadcasted_iota(jnp.int32, (1, 256), 1) // HD
    return [(slot == first + i).astype(F32).astype(BF) for i in range(count)]


def stack_heads(block, masks):
    return jnp.concatenate([block * mask for mask in masks], axis=0)


def pick_heads(stacked, masks, size):
    total = None
    for i, mask in enumerate(masks):
        part = stacked[i * size : (i + 1) * size] * mask.astype(F32)
        total = part if total is None else total + part
    return total


def norm_forward(value, gain, shift):
    average = jnp.mean(value, axis=-1, keepdims=True)
    centered = value - average
    variance = jnp.mean(centered * centered, axis=-1, keepdims=True)
    scaled = lax.rsqrt(variance + EPS)
    unit = centered * scaled
    return unit * gain + shift, unit, scaled


def norm_back(grad, unit, scaled, gain):
    inner = grad * gain
    centered = inner - jnp.mean(inner, axis=-1, keepdims=True)
    return scaled * (centered - unit * jnp.mean(inner * unit, axis=-1, keepdims=True))


def attn_fwd_kernel(
    rows, win_ref, own_ref, g_ref, qb_ref, kvb_ref, qseg_ref, kseg_ref, vec_ref,
    q_ref, kv_ref, ctx_ref, mid_ref, unit_ref, rs_ref, acc_ref,
):
    step = pl.program_id(0)
    tokens = own_ref.shape[0]
    heads = 3
    kv_ref[0] = (dot(win_ref[...], g_ref[0, :, 384:768]) + kvb_ref[0]).astype(BF)
    q_ref[0] = (dot(own_ref[...].astype(BF), g_ref[0, :, 0:256]) + qb_ref[0]).astype(BF)
    q_masks, c_masks = lane_masks(0, heads), lane_masks(1, heads)
    for j, slot in enumerate(window_slots(tokens, rows)):
        here = pl.ds(j * BLK, BLK)
        keys = pl.ds(pl.multiple_of(slot * PACK, PACK), PACK)
        stacked = stack_heads(q_ref[0, here, :], q_masks)
        scores = dot_nt(stacked, kv_ref[0, keys, 0:256]) * (HD**-0.5)
        kseg = jnp.where(slot == 0, kseg_ref[0:1], kseg_ref[1:2])
        qseg = qseg_ref[here, :]
        allowed = jnp.logical_and(kseg >= 0, jnp.logical_or(kseg == qseg, qseg < 0))
        allowed = jnp.concatenate([allowed] * heads, axis=0)
        scores = jnp.where(allowed, scores, NEG)
        peak = jnp.max(scores, axis=-1, keepdims=True)
        weights = jnp.exp(scores - peak)
        probs = weights * (1.0 / jnp.sum(weights, axis=-1, keepdims=True))
        out = dot(probs.astype(BF), kv_ref[0, keys, 128:384])
        ctx_ref[0, here, :] = pick_heads(out, c_masks, BLK).astype(BF)
    part = dot_nt(ctx_ref[0], g_ref[0, :, 128:384])

    @pl.when(step == 0)
    def _():
        acc_ref[...] = part

    @pl.when(step > 0)
    def _():
        acc_ref[...] += part

    @pl.when(step == pl.num_programs(0) - 1)
    def _():
        total = own_ref[...].astype(F32) + acc_ref[...] + vec_ref[0:1]
        mid_ref[...], unit_ref[...], rs_ref[...] = norm_forward(total, vec_ref[1:2], vec_ref[2:3])


def attn_fwd(win, own, g, qb, kvb, qseg, kseg, vec, rows):
    n, tokens, dim = g.shape[0], own.shape[0], own.shape[1]
    last = g.shape[2] // dim - 1
    return pl.pallas_call(
        functools.partial(attn_fwd_kernel, rows),
        grid=(n,),
        in_specs=[
            whole(win.shape), whole(own.shape), per_t((1, dim, dim), 0, last),
            per_t((1, 1, 256)), per_t((1, 1, 384)), whole(qseg.shape), whole(kseg.shape), whole(vec.shape),
        ],
        out_specs=[
            per_t((1, tokens, 256)), per_t((1, WIN, 384)), per_t((1, tokens, 256)),
            whole((tokens, dim)), whole((tokens, dim)), whole((tokens, 1)),
        ],
        out_shape=[
            jax.ShapeDtypeStruct((n, tokens, 256), BF), jax.ShapeDtypeStruct((n, WIN, 384), BF),
            jax.ShapeDtypeStruct((n, tokens, 256), BF), jax.ShapeDtypeStruct((tokens, dim), F32),
            jax.ShapeDtypeStruct((tokens, dim), F32), jax.ShapeDtypeStruct((tokens, 1), F32),
        ],
        scratch_shapes=[pltpu.VMEM((tokens, dim), F32)],
        compiler_params=params(),
        name="attn_fwd",
    )(win, own, g, qb, kvb, qseg, kseg, vec)


def ffn_fwd_kernel(
    mid_ref, up_ref, down_ref, ub_ref, vec_ref, act_ref, slope_ref, out_ref, low_ref, unit_ref, rs_ref, acc_ref
):
    step = pl.program_id(0)
    upper = dot(mid_ref[...].astype(BF), up_ref[0]) + ub_ref[0]
    half = 0.5 + 0.5 * lax.erf(upper * (0.5**0.5))
    act_ref[0] = (upper * half).astype(BF)
    slope_ref[0] = (half + upper * (jnp.exp(-0.5 * upper * upper) * 0.3989422804014327)).astype(BF)
    part = dot_nt(act_ref[0], down_ref[0])

    @pl.when(step == 0)
    def _():
        acc_ref[...] = part

    @pl.when(step > 0)
    def _():
        acc_ref[...] += part

    @pl.when(step == pl.num_programs(0) - 1)
    def _():
        total = mid_ref[...] + acc_ref[...] + vec_ref[3:4]
        out, unit_ref[...], rs_ref[...] = norm_forward(total, vec_ref[4:5], vec_ref[5:6])
        out_ref[...] = out
        low_ref[...] = out.astype(BF)


def ffn_fwd(mid, g, ub, vec):
    n, (tokens, dim) = g.shape[0], mid.shape
    return pl.pallas_call(
        ffn_fwd_kernel,
        grid=(n,),
        in_specs=[
            whole(mid.shape), per_t((1, dim, dim), 0, 0), per_t((1, dim, dim), 0, 1), per_t((1, 1, dim)), whole(vec.shape),
        ],
        out_specs=[
            per_t((1, tokens, dim)), per_t((1, tokens, dim)),
            whole((tokens, dim)), whole((tokens, dim)), whole((tokens, dim)), whole((tokens, 1)),
        ],
        out_shape=[
            jax.ShapeDtypeStruct((n, tokens, dim), BF), jax.ShapeDtypeStruct((n, tokens, dim), BF),
            jax.ShapeDtypeStruct((tokens, dim), F32), jax.ShapeDtypeStruct((tokens, dim), BF),
            jax.ShapeDtypeStruct((tokens, dim), F32), jax.ShapeDtypeStruct((tokens, 1), F32),
        ],
        scratch_shapes=[pltpu.VMEM((tokens, dim), F32)],
        compiler_params=params(),
        name="ffn_fwd",
    )(mid, g, g, ub, vec)


def column_sum(value):
    return jnp.sum(value, axis=0, keepdims=True)


def ffn_bwd_kernel(
    grad_ref, mid_ref, unit2_ref, rs2_ref, unit1_ref, rs1_ref, up_ref, down_ref, act_ref, slope_ref, vec_ref,
    dg_ref, ub_ref, dvec_ref, dfirst_ref, acc_ref, low_ref, low_t_ref, mid_t_ref,
):
    step = pl.program_id(0)
    dim = grad_ref.shape[1]

    @pl.when(step == 0)
    def _():
        grad = grad_ref[...]
        dsecond = norm_back(grad, unit2_ref[...], rs2_ref[...], vec_ref[4:5])
        dvec_ref[4:5] = column_sum(grad * unit2_ref[...])
        dvec_ref[5:6] = column_sum(grad)
        dvec_ref[3:4] = column_sum(dsecond)
        dvec_ref[6:8] = jnp.zeros((2, dim), F32)
        acc_ref[...] = dsecond
        low_ref[...] = dsecond.astype(BF)
        low_t_ref[...] = dsecond.T.astype(BF)
        mid_t_ref[...] = mid_ref[...].T.astype(BF)

    dupper = dot(low_ref[...], down_ref[0]) * slope_ref[0].astype(F32)
    ub_ref[0] = column_sum(dupper)
    dupper_low = dupper.astype(BF)
    dg_ref[0, :, 0:dim] = dot(mid_t_ref[...], dupper_low).astype(BF)
    dg_ref[0, :, dim : 2 * dim] = dot(low_t_ref[...], act_ref[0]).astype(BF)
    acc_ref[...] += dot_nt(dupper_low, up_ref[0])

    @pl.when(step == pl.num_programs(0) - 1)
    def _():
        dmid = acc_ref[...]
        dfirst = norm_back(dmid, unit1_ref[...], rs1_ref[...], vec_ref[1:2])
        dvec_ref[1:2] = column_sum(dmid * unit1_ref[...])
        dvec_ref[2:3] = column_sum(dmid)
        dvec_ref[0:1] = column_sum(dfirst)
        dfirst_ref[...] = dfirst


def ffn_bwd(grad, mid, unit2, rs2, unit1, rs1, g, act, slope, vec):
    n, (tokens, dim) = g.shape[0], mid.shape
    full = whole((tokens, dim))
    return pl.pallas_call(
        ffn_bwd_kernel,
        grid=(n,),
        in_specs=[
            full, full, full, whole((tokens, 1)), full, whole((tokens, 1)),
            per_t((1, dim, dim), 0, 0), per_t((1, dim, dim), 0, 1),
            per_t((1, tokens, dim)), per_t((1, tokens, dim)), whole(vec.shape),
        ],
        out_specs=[per_t((1, dim, 2 * dim), 0, 0), per_t((1, 1, dim)), whole((8, dim)), full],
        out_shape=[
            jax.ShapeDtypeStruct(g.shape, BF), jax.ShapeDtypeStruct((n, 1, dim), F32),
            jax.ShapeDtypeStruct((8, dim), F32), jax.ShapeDtypeStruct((tokens, dim), F32),
        ],
        scratch_shapes=[
            pltpu.VMEM((tokens, dim), F32), pltpu.VMEM((tokens, dim), BF),
            pltpu.VMEM((dim, tokens), BF), pltpu.VMEM((dim, tokens), BF),
        ],
        compiler_params=params(),
        name="ffn_bwd",
    )(grad, mid, unit2, rs2, unit1, rs1, g, g, act, slope, vec)


def attn_bwd_kernel(
    rows, dg_in, dfirst_ref, own_ref, win_ref, g_ref, q_ref, kv_ref, ctx_ref, qseg_ref, kseg_ref,
    dg_ref, qb_ref, vb_ref, own_grad_ref, win_grad_ref, low_ref, low_t_ref, own_t_ref, win_t_ref, dctx_ref, dq_ref, dkv_ref,
):
    step = pl.program_id(0)
    tokens = own_ref.shape[0]
    heads = 3

    @pl.when(step == 0)
    def _():
        dfirst = dfirst_ref[...]
        low_ref[...] = dfirst.astype(BF)
        low_t_ref[...] = dfirst.T.astype(BF)
        own_t_ref[...] = own_ref[...].astype(F32).T.astype(BF)
        win_t_ref[...] = win_ref[...].astype(F32).T.astype(BF)
        own_grad_ref[...] = dfirst
        win_grad_ref[...] = jnp.zeros(win_grad_ref.shape, F32)

    dctx_ref[...] = dot(low_ref[...], g_ref[0, :, 128:384]).astype(BF)
    dkv_ref[...] = jnp.zeros(dkv_ref.shape, F32)
    q_masks, c_masks = lane_masks(0, heads), lane_masks(1, heads)
    for j, slot in enumerate(window_slots(tokens, rows)):
        here = pl.ds(j * BLK, BLK)
        keys = pl.ds(pl.multiple_of(slot * PACK, PACK), PACK)
        q_stack = stack_heads(q_ref[0, here, :], q_masks)
        d_stack = stack_heads(dctx_ref[here, :], c_masks)
        scores = dot_nt(kv_ref[0, keys, 0:256], q_stack) * (HD**-0.5)
        kseg = kseg_ref[keys, :]
        qseg = qseg_ref[j : j + 1, :]
        allowed = jnp.logical_and(kseg >= 0, jnp.logical_or(kseg == qseg, qseg < 0))
        allowed = jnp.concatenate([allowed] * heads, axis=1)
        scores = jnp.where(allowed, scores, NEG)
        peak = jnp.max(scores, axis=0, keepdims=True)
        weights = jnp.exp(scores - peak)
        probs = weights * (1.0 / jnp.sum(weights, axis=0, keepdims=True))
        dprobs = dot_nt(kv_ref[0, keys, 128:384], d_stack)
        weighted = probs * dprobs
        inner = jnp.sum(weighted, axis=0, keepdims=True)
        dscores = ((weighted - probs * inner) * (HD**-0.5)).astype(BF)
        dkv_ref[keys, 128:384] += dot(probs.astype(BF), d_stack)
        dkv_ref[keys, 0:256] += dot(dscores, q_stack)
        dq_ref[here, :] = pick_heads(dot_tn(dscores, kv_ref[0, keys, 0:256]), q_masks, BLK)
    dq, dkv = dq_ref[...], dkv_ref[...]
    qb_ref[0] = column_sum(dq)
    vb_ref[0] = column_sum(dkv)
    dq_low, dkv_low = dq.astype(BF), dkv.astype(BF)
    grad_q = dot(own_t_ref[...], dq_low)
    grad_o = dot(low_t_ref[...], ctx_ref[0])
    dg_ref[0, :, 0:128] = grad_q[:, 0:128].astype(BF)
    dg_ref[0, :, 128:256] = (grad_q[:, 128:256] + grad_o[:, 0:128]).astype(BF)
    dg_ref[0, :, 256:384] = grad_o[:, 128:256].astype(BF)
    dg_ref[0, :, 384:768] = dot(win_t_ref[...], dkv_low).astype(BF)
    own_grad_ref[...] += dot_nt(dq_low, g_ref[0, :, 0:256])
    win_grad_ref[...] += dot_nt(dkv_low, g_ref[0, :, 384:768])


def attn_bwd(dg, dfirst, own, win, g, q, kv, ctx, qseg, kseg, rows):
    n, (tokens, dim) = g.shape[0], own.shape
    last = g.shape[2] // dim - 1
    return pl.pallas_call(
        functools.partial(attn_bwd_kernel, rows),
        grid=(n,),
        in_specs=[
            pl.BlockSpec(memory_space=pl.ANY), whole((tokens, dim)), whole((tokens, dim)), whole(win.shape),
            per_t((1, dim, dim), 0, last), per_t((1, tokens, 256)), per_t((1, WIN, 384)), per_t((1, tokens, 256)),
            whole(qseg.shape), whole(kseg.shape),
        ],
        out_specs=[
            per_t((1, dim, dim), 0, last), per_t((1, 1, 256)), per_t((1, 1, 384)),
            whole((tokens, dim)), whole((WIN, dim)),
        ],
        out_shape=[
            jax.ShapeDtypeStruct(dg.shape, BF), jax.ShapeDtypeStruct((n, 1, 256), F32),
            jax.ShapeDtypeStruct((n, 1, 384), F32), jax.ShapeDtypeStruct((tokens, dim), F32),
            jax.ShapeDtypeStruct((WIN, dim), F32),
        ],
        scratch_shapes=[
            pltpu.VMEM((tokens, dim), BF), pltpu.VMEM((dim, tokens), BF), pltpu.VMEM((dim, tokens), BF),
            pltpu.VMEM((dim, WIN), BF), pltpu.VMEM((tokens, 256), BF), pltpu.VMEM((tokens, 256), F32),
            pltpu.VMEM((WIN, 384), F32),
        ],
        input_output_aliases={0: 0},
        compiler_params=params(),
        name="attn_bwd",
    )(dg, dfirst, own, win, g, q, kv, ctx, qseg, kseg)


def body(n_dp, n_tensor, block_input, passage_lengths, qkv_weight, qv_bias, out_weight, out_bias, first_gain,
         first_shift, up_weight, up_bias, down_weight, down_bias, second_gain, second_shift, output_grad):
    layers = qkv_weight.shape[0]
    tokens, dim = block_input.shape
    rows, segments = passage_lengths.shape
    t = lax.axis_index("tensor")
    dp = lax.axis_index("dp")
    shard, units = qkv_weight.shape[2], qkv_weight.shape[3]
    hidden_units = up_weight.shape[2]

    packs = [
        jnp.concatenate(
            [up_weight[l], down_weight[l].T, qkv_weight[l, 0], out_weight[l].T, qkv_weight[l, 1], qkv_weight[l, 2]], axis=1
        )
        for l in range(layers)
    ]
    small = jnp.concatenate([qv_bias.reshape(layers, -1), up_bias], axis=1)
    small = lax.all_gather(small, ("tensor", "dp"), axis=0).astype(F32)
    small = small.reshape(n_tensor, n_dp, layers, -1)
    piece = qv_bias.shape[2]
    qv = small[..., : 2 * piece].reshape(n_tensor, n_dp, layers, 2, piece).transpose(2, 3, 0, 1, 4)
    qv = qv.reshape(layers, 2, n_tensor, 1, units)
    q_bias = jnp.pad(qv[:, 0], ((0, 0), (0, 0), (0, 0), (0, 256 - units)))
    kv_bias = jnp.pad(qv[:, 1], ((0, 0), (0, 0), (0, 0), (units, 0)))
    u_bias = small[..., 2 * piece :].transpose(2, 0, 1, 3).reshape(layers, n_tensor, 1, hidden_units)

    zero = jnp.zeros((1, dim), F32)
    vecs = [
        jnp.concatenate(
            [v[l : l + 1] for v in (out_bias, first_gain, first_shift, down_bias, second_gain, second_shift)] + [zero, zero],
            axis=0,
        )
        for l in range(layers)
    ]

    ends = jnp.cumsum(passage_lengths, axis=1, dtype=jnp.int32)
    places = jnp.arange(PACK, dtype=jnp.int32)
    seg = jnp.sum((places[None, :, None] >= ends[:, None, :]).astype(jnp.int32), axis=2, dtype=jnp.int32)
    seg = jnp.where(seg == segments, -1, seg)
    first_row = jnp.minimum(t * tokens // PACK, rows - 2)
    kseg = lax.dynamic_slice(seg, (first_row, 0), (2, PACK))
    kcol = kseg.reshape(WIN, 1)
    qseg = lax.dynamic_slice(seg.reshape(-1), (t * tokens,), (tokens,))
    qcol = qseg.reshape(tokens, 1)
    qrow = qseg.reshape(tokens // BLK, BLK)

    pad = PACK // 2
    start = pad + first_row * PACK - (t - 1) * tokens
    up = [(i, i + 1) for i in range(n_tensor - 1)]
    down = [(i + 1, i) for i in range(n_tensor - 1)]
    edge = jnp.zeros((pad, dim), BF)

    def window(low):
        before = lax.ppermute(low, "tensor", up)
        after = lax.ppermute(low, "tensor", down)
        line = jnp.concatenate([edge, before, low, after, edge], axis=0)
        return lax.dynamic_slice(line, (start, 0), (WIN, dim))

    def window_back(own_grad, win_grad):
        line = lax.dynamic_update_slice(jnp.zeros((2 * pad + 3 * tokens, dim), F32), win_grad, (start, 0))
        before = lax.ppermute(line[pad : pad + tokens].astype(BF), "tensor", down)
        after = lax.ppermute(line[pad + 2 * tokens : pad + 3 * tokens].astype(BF), "tensor", up)
        return own_grad + line[pad + tokens : pad + 2 * tokens] + before.astype(F32) + after.astype(F32)

    own, win = block_input, window(block_input)
    kept = []
    for l in range(layers):
        g = gather_weights(packs[l], n_dp, n_tensor, 0)
        q, kv, ctx, mid, unit1, rs1 = attn_fwd(win, own, g, q_bias[l], kv_bias[l], qcol, kseg, vecs[l], rows)
        act, slope, out, low, unit2, rs2 = ffn_fwd(mid, g, u_bias[l], vecs[l])
        kept.append((own, win, g, q, kv, ctx, mid, unit1, rs1, act, slope, unit2, rs2))
        own = out
        if l < layers - 1:
            win = window(low)
    block_output = own

    grad = output_grad
    pieces, smalls = [None] * layers, [None] * layers
    for l in reversed(range(layers)):
        own, win, g, q, kv, ctx, mid, unit1, rs1, act, slope, unit2, rs2 = kept[l]
        dg, ub, dvec, dfirst = ffn_bwd(grad, mid, unit2, rs2, unit1, rs1, g, act, slope, vecs[l])
        dg, qb, vb, own_grad, win_grad = attn_bwd(dg, dfirst, own, win, g, q, kv, ctx, qrow, kcol, rows)
        grad = window_back(own_grad, win_grad)
        pieces[l] = scatter_grads(dg, n_dp, n_tensor, 1)
        smalls[l] = jnp.concatenate(
            [dvec[:6].reshape(-1), qb[:, 0, :units].reshape(-1), vb[:, 0, units:].reshape(-1), ub.reshape(-1)]
        )
    totals = lax.psum(jnp.stack(smalls), ("dp", "tensor"))
    vec_totals = totals[:, : 6 * dim].reshape(layers, 6, dim)
    qv_totals = totals[:, 6 * dim : 6 * dim + 2 * n_tensor * units].reshape(layers, 2, n_tensor * units)
    u_totals = totals[:, 6 * dim + 2 * n_tensor * units :]
    qv_grad = lax.dynamic_slice(qv_totals, (0, 0, (t * n_dp + dp) * piece), (layers, 2, piece))
    wide = up_bias.shape[1]
    u_grad = lax.dynamic_slice(u_totals, (0, (t * n_dp + dp) * wide), (layers, wide))

    both = jnp.stack(pieces)
    base = 2 * hidden_units
    cols = [both[:, :, base + i * units : base + (i + 1) * units] for i in range(4)]
    return (
        block_output,
        grad,
        jnp.stack([cols[0], cols[2], cols[3]], axis=1),
        qv_grad,
        cols[1].transpose(0, 2, 1),
        vec_totals[:, 0],
        vec_totals[:, 1],
        vec_totals[:, 2],
        both[:, :, :hidden_units],
        u_grad,
        both[:, :, hidden_units:base].transpose(0, 2, 1),
        vec_totals[:, 3],
        vec_totals[:, 4],
        vec_totals[:, 5],
    )


def solution(mesh):
    n_dp, n_tensor = mesh.shape["dp"], mesh.shape["tensor"]
    tokens = P(("dp", "tensor"), None)
    in_specs = (
        tokens, P("dp", None), P(None, None, "dp", "tensor"), P(None, None, ("tensor", "dp")), P(None, "tensor", "dp"),
        P(), P(), P(), P(None, "dp", "tensor"), P(None, ("tensor", "dp")), P(None, "tensor", "dp"), P(), P(), P(), tokens,
    )
    out_specs = (
        tokens, tokens, P(None, None, "dp", "tensor"), P(None, None, ("tensor", "dp")), P(None, "tensor", "dp"),
        P(), P(), P(), P(None, "dp", "tensor"), P(None, ("tensor", "dp")), P(None, "tensor", "dp"), P(), P(), P(),
    )
    return jax.shard_map(
        functools.partial(body, n_dp, n_tensor), mesh=mesh, in_specs=in_specs, out_specs=out_specs, check_vma=False
    )
```

```python
import functools

import jax
import jax.numpy as jnp
from jax import lax
from jax.experimental import pallas as pl
from jax.experimental.pallas import tpu as pltpu
from jax.sharding import PartitionSpec as P

HD = 64
PACK = 512
BLK = 128
WIN = 2 * PACK
EPS = 1e-05
NEG = -1e30
MESH = pl.DeviceIdType.MESH
BF = jnp.bfloat16
F32 = jnp.float32


def dot(a, b):
    return jnp.dot(a, b, preferred_element_type=F32)


def dot_nt(a, b):
    return lax.dot_general(a, b, (((1,), (1,)), ((), ())), preferred_element_type=F32)


def dot_tn(a, b):
    return lax.dot_general(a, b, (((0,), (0,)), ((), ())), preferred_element_type=F32)


def params(**kw):
    return pltpu.CompilerParams(vmem_limit_bytes=60 * 1024 * 1024, **kw)


def whole(shape):
    return pl.BlockSpec(shape, lambda t: (0,) * len(shape))


def per_t(shape, *rest):
    tail = rest if rest else (0,) * (len(shape) - 1)
    return pl.BlockSpec(shape, lambda t: (t,) + tail)


class Place:
    def __init__(self, n_dp):
        self.nz = n_dp // 2
        dp, tensor = lax.axis_index("dp"), lax.axis_index("tensor")
        self.dp, self.tensor = dp, tensor
        self.z, self.y = dp // 2, dp % 2
        self.x, self.c = tensor // 2, tensor % 2
        self.dp_y = 2 * self.z + 1 - self.y
        self.t_x = 2 * (1 - self.x) + self.c
        self.t_c = 2 * self.x + 1 - self.c
        self.t_xc = 2 * (1 - self.x) + 1 - self.c
        self.to_x = (dp, self.t_x)
        self.to_y = (self.dp_y, tensor)
        self.to_c = (dp, self.t_c)

    def d(self, z, same_y=True):
        return 2 * z + (self.y if same_y else 1 - self.y)


def greet(devices):
    barrier = pltpu.get_barrier_semaphore()
    for device in devices:
        pl.semaphore_signal(barrier, inc=1, device_id=device, device_id_type=MESH)
    pl.semaphore_wait(barrier, len(devices))


def bits(n):
    return n.bit_length() - 1


def pairs(me, n_dp, n_tensor):
    found = [(me.dp, me.tensor ^ (1 << b)) for b in range(bits(n_tensor))]
    return found + [(me.dp ^ (1 << b), me.tensor) for b in range(bits(n_dp))]


def doubling_gather(me, n_dp, n_tensor, own_ref, all_ref, own_sem, send_sem, recv_sem):
    held = []
    for b in range(bits(n_tensor)):
        size = 1 << b
        held.append(all_ref.at[pl.ds(me.tensor // size * size, size), me.dp])
    for b in range(bits(n_dp)):
        size = 1 << b
        held.append(all_ref.at[:, pl.ds(me.dp // size * size, size)])
    copies = [
        pltpu.make_async_remote_copy(
            src_ref=block, dst_ref=block, send_sem=send_sem.at[i], recv_sem=recv_sem.at[i],
            device_id=device, device_id_type=MESH,
        )
        for i, (block, device) in enumerate(zip(held, pairs(me, n_dp, n_tensor)))
    ]
    mine = pltpu.make_async_copy(own_ref, all_ref.at[me.tensor, me.dp], own_sem)

    def begin():
        mine.start()
        mine.wait()
        copies[0].start()

    def middle(i):
        copies[i].wait_recv()
        if i + 1 < len(copies):
            copies[i + 1].start()

    def end():
        for copy in copies:
            copy.wait_send()

    return [begin] + [functools.partial(middle, i) for i in range(len(copies))] + [end]


def doubling_sum(me, n_dp, n_tensor, own_ref, total_ref, part_ref, come_ref, send_sem, recv_sem):
    devices = pairs(me, n_dp, n_tensor)
    copies = [
        pltpu.make_async_remote_copy(
            src_ref=part_ref.at[i], dst_ref=come_ref.at[i], send_sem=send_sem.at[i], recv_sem=recv_sem.at[i],
            device_id=device, device_id_type=MESH,
        )
        for i, device in enumerate(devices)
    ]

    def begin():
        part_ref[0] = own_ref[...]
        copies[0].start()

    def middle(i):
        copies[i].wait_recv()
        total = part_ref[i] + come_ref[i]
        if i + 1 < len(copies):
            part_ref[i + 1] = total
            copies[i + 1].start()
        else:
            total_ref[...] = total

    def end():
        for copy in copies:
            copy.wait_send()

    return [begin] + [functools.partial(middle, i) for i in range(len(copies))] + [end]


def gather_kernel(n_dp, n_tensor, small, *refs):
    if small:
        own_ref, few_ref, out_ref, few_out_ref, own_sem, send_sem, recv_sem, few_sem, few_send, few_recv = refs
    else:
        own_ref, out_ref, own_sem, send_sem, recv_sem = refs
    me = Place(n_dp)
    nz = me.nz
    half = own_ref.shape[1] // 2
    barrier = pltpu.get_barrier_semaphore()
    far = [(me.dp ^ (2 << b), me.tensor) for b in range(1, bits(nz))] if small else []
    for device in far:
        pl.semaphore_signal(barrier, inc=1, device_id=device, device_id_type=MESH)
    for device in (me.to_x, me.to_y, me.to_c):
        pl.semaphore_signal(barrier, inc=1, device_id=device, device_id_type=MESH)

    @pl.when(me.z > 0)
    def _():
        pl.semaphore_signal(barrier, inc=1, device_id=(me.dp - 2, me.tensor), device_id_type=MESH)

    @pl.when(me.z < nz - 1)
    def _():
        pl.semaphore_signal(barrier, inc=1, device_id=(me.dp + 2, me.tensor), device_id_type=MESH)

    pl.semaphore_wait(barrier, 3 + len(far) + (me.z > 0).astype(jnp.int32) + (me.z < nz - 1).astype(jnp.int32))
    rounds = doubling_gather(me, n_dp, n_tensor, few_ref, few_out_ref, few_sem, few_send, few_recv) if small else []

    def piece(t, d, part):
        if part is None:
            return out_ref.at[t, d]
        return out_ref.at[t, d, :, pl.ds(part * half, half)]

    def copy(source, t, d, part, route, z, device):
        slot = route * nz + z
        return pltpu.make_async_remote_copy(
            src_ref=source if source is not None else piece(t, d, part),
            dst_ref=piece(t, d, part),
            send_sem=send_sem.at[slot],
            recv_sem=recv_sem.at[slot],
            device_id=device,
            device_id_type=MESH,
        )

    mine = pltpu.make_async_copy(own_ref, out_ref.at[me.tensor, me.dp], own_sem)
    mine.start()

    def z_copy(p, up, source=None):
        return copy(source, me.tensor, me.d(p), None, 0, p, (me.dp + 2 if up else me.dp - 2, me.tensor))

    def x_copy(p, source=None):
        return copy(source, me.tensor, me.d(p), None, 1, p, me.to_x)

    def y_copy(p, source=None):
        return copy(source, me.tensor, me.d(p), None, 2, p, me.to_y)

    def first_copy(p):
        return copy(None, me.t_x, me.d(p), 0, 3, p, me.to_y)

    def second_copy(p):
        return copy(None, me.tensor, me.d(p, False), 1, 4, p, me.to_x)

    def core_copy(kind, p, source=None):
        t = me.tensor if kind in (0, 2) else me.t_x
        d = me.d(p, kind in (0, 1))
        part = {3: 0, 4: 1}.get(kind)
        return copy(source, t, d, part, 5 + kind, p, me.to_c)

    def arrived(t, d, part, slot):
        pltpu.make_async_copy(piece(t, d, part), piece(t, d, part), recv_sem.at[slot]).wait()

    def own_round():
        @pl.when(me.z < nz - 1)
        def _():
            z_copy(me.z, True, own_ref).start()

        @pl.when(me.z > 0)
        def _():
            copy(own_ref, me.tensor, me.dp, None, 10, me.z, (me.dp - 2, me.tensor)).start()

        x_copy(me.z, own_ref).start()
        y_copy(me.z, own_ref).start()
        core_copy(0, me.z, own_ref).start()

    def z_round(p, up, valid):
        @pl.when(valid)
        def _():
            arrived(me.tensor, me.d(p), None, (0 if up else 10) * nz + p)

            @pl.when(me.z < nz - 1 if up else me.z > 0)
            def _():
                if up:
                    z_copy(p, True).start()
                else:
                    copy(None, me.tensor, me.d(p), None, 10, p, (me.dp - 2, me.tensor)).start()

            x_copy(p).start()
            y_copy(p).start()
            core_copy(0, p).start()

    def xy_round(p, valid):
        @pl.when(valid)
        def _():
            arrived(me.t_x, me.d(p), None, nz + p)
            first_copy(p).start()
            core_copy(1, p).start()
            arrived(me.tensor, me.d(p, False), None, 2 * nz + p)
            second_copy(p).start()
            core_copy(2, p).start()

    def diagonal_round(p, valid):
        @pl.when(valid)
        def _():
            arrived(me.t_x, me.d(p, False), 0, 3 * nz + p)
            core_copy(3, p).start()
            arrived(me.t_x, me.d(p, False), 1, 4 * nz + p)
            core_copy(4, p).start()

    true = me.z >= 0
    own_round()
    for s in range(1, nz + 2):
        if rounds:
            rounds.pop(0)()
        if s < nz:
            z_round(me.z - s, True, me.z - s >= 0)
            z_round(me.z + s, False, me.z + s < nz)
        if s == 1:
            xy_round(me.z, true)
        elif s - 1 < nz:
            xy_round(me.z - s + 1, me.z - s + 1 >= 0)
            xy_round(me.z + s - 1, me.z + s - 1 < nz)
        if s == 2:
            diagonal_round(me.z, true)
        elif 2 < s < nz + 2:
            diagonal_round(me.z - s + 2, me.z - s + 2 >= 0)
            diagonal_round(me.z + s - 2, me.z + s - 2 < nz)

    for turn in rounds:
        turn()

    for p in range(nz):
        for kind in range(5):
            t = me.t_c if kind in (0, 2) else me.t_xc
            part = {3: 0, 4: 1}.get(kind)
            arrived(t, me.d(p, kind in (0, 1)), part, (5 + kind) * nz + p)

    mine.wait()
    for p in range(nz):
        @pl.when(jnp.logical_and(me.z < nz - 1, p <= me.z))
        def _():
            z_copy(p, True).wait_send()

        @pl.when(jnp.logical_and(me.z > 0, p >= me.z))
        def _():
            copy(None, me.tensor, me.d(p), None, 10, p, (me.dp - 2, me.tensor)).wait_send()

        x_copy(p).wait_send()
        y_copy(p).wait_send()
        first_copy(p).wait_send()
        second_copy(p).wait_send()
        for kind in range(5):
            core_copy(kind, p).wait_send()


def gather_weights(own, few, n_dp, n_tensor, collective_id):
    rows, cols = own.shape
    slots = 11 * (n_dp // 2)
    small = few is not None
    rounds = bits(n_dp) + bits(n_tensor)
    hbm = pl.BlockSpec(memory_space=pltpu.MemorySpace.HBM)
    vmem = pl.BlockSpec(memory_space=pltpu.MemorySpace.VMEM)
    out_shape = [jax.ShapeDtypeStruct((n_tensor, n_dp, rows, cols), own.dtype)]
    scratch = [pltpu.SemaphoreType.DMA, pltpu.SemaphoreType.DMA((slots,)), pltpu.SemaphoreType.DMA((slots,))]
    if small:
        out_shape.append(jax.ShapeDtypeStruct((n_tensor, n_dp) + few.shape, few.dtype))
        scratch += [pltpu.SemaphoreType.DMA, pltpu.SemaphoreType.DMA((rounds,)), pltpu.SemaphoreType.DMA((rounds,))]
    out = pl.pallas_call(
        functools.partial(gather_kernel, n_dp, n_tensor, small),
        out_shape=out_shape,
        in_specs=[hbm, vmem] if small else [hbm],
        out_specs=[hbm, vmem] if small else [hbm],
        scratch_shapes=scratch,
        compiler_params=pltpu.CompilerParams(collective_id=collective_id, has_side_effects=True),
        name="gather_weights",
    )(*([own, few] if small else [own]))
    return (out[0].reshape(n_tensor, n_dp * rows, cols),) + tuple(out[1:])


def scatter_kernel(n_dp, n_tensor, small, *refs):
    if small:
        g_ref, few_ref, out_ref, few_out_ref, *refs, few_part, few_come, few_send, few_recv = refs
    else:
        g_ref, out_ref, *refs = refs
    mine, core_in, first_in, second_in, x_in, y_in, z_in, load_sem, send_sem, recv_sem = refs
    me = Place(n_dp)
    nz = me.nz
    cols = g_ref.shape[-1]
    half = cols // 2
    zs = [lax.rem(me.z + k, nz) for k in range(1, nz)] + [me.z]
    peers = [me.to_x, me.to_y, me.to_c] + [(me.d(z), me.tensor) for z in zs[:-1]]
    greet(peers)

    def owner(place, k):
        x_other, y_other = place in (0, 1), place in (0, 2)
        return x_other, me.d(zs[k], not y_other)

    def remote(source, target, slot, device):
        return pltpu.make_async_remote_copy(
            src_ref=source, dst_ref=target, send_sem=send_sem.at[slot], recv_sem=recv_sem.at[slot],
            device_id=device, device_id_type=MESH,
        )

    def to_core(place, k):
        x_other, d = owner(place, k)
        return remote(g_ref.at[me.t_xc if x_other else me.t_c, d], core_in.at[place, k], place * nz + k, me.to_c)

    def load(place, k):
        x_other, d = owner(place, k)
        return pltpu.make_async_copy(
            g_ref.at[me.t_x if x_other else me.tensor, d], mine.at[place, k], load_sem.at[place * nz + k]
        )

    for k in range(nz):
        for place in range(4):
            to_core(place, k).start()
            load(place, k).start()
    rounds = []
    if small:
        rounds = doubling_sum(me, n_dp, n_tensor, few_ref, few_out_ref, few_part, few_come, few_send, few_recv)

    def first(k):
        return remote(mine.at[0, k, :, pl.ds(0, half)], first_in.at[k], 4 * nz + k, me.to_x)

    def second(k):
        return remote(mine.at[0, k, :, pl.ds(half, half)], second_in.at[k], 5 * nz + k, me.to_y)

    def along_x(k):
        return remote(mine.at[1, k], x_in.at[k], 6 * nz + k, me.to_x)

    def along_y(k):
        return remote(mine.at[2, k], y_in.at[k], 7 * nz + k, me.to_y)

    def along_z(k):
        return remote(mine.at[3, k], z_in.at[k], 8 * nz + k, (me.d(zs[k]), me.tensor))

    def both(place, k):
        load(place, k).wait()
        to_core(place, k).wait_recv()
        return mine[place, k].astype(F32) + core_in[place, k].astype(F32)

    for step in range(nz + 2):
        if rounds:
            rounds.pop(0)()
        if step < nz:
            k = step
            mine[0, k] = both(0, k).astype(BF)
            first(k).start()
            second(k).start()
        if 0 <= step - 1 < nz:
            k = step - 1
            total = both(1, k)
            second(k).wait_recv()
            mine[1, k, :, :half] = total[:, :half].astype(BF)
            mine[1, k, :, half:] = (total[:, half:] + second_in[k].astype(F32)).astype(BF)
            along_x(k).start()
            total = both(2, k)
            first(k).wait_recv()
            mine[2, k, :, half:] = total[:, half:].astype(BF)
            mine[2, k, :, :half] = (total[:, :half] + first_in[k].astype(F32)).astype(BF)
            along_y(k).start()
        if 0 <= step - 2 < nz:
            k = step - 2
            total = both(3, k)
            along_x(k).wait_recv()
            total += x_in[k].astype(F32)
            along_y(k).wait_recv()
            total += y_in[k].astype(F32)
            if k < nz - 1:
                mine[3, k] = total.astype(BF)
                along_z(k).start()
            else:
                for j in range(nz - 1):
                    along_z(j).wait_recv()
                    total += z_in[j].astype(F32)
                out_ref[...] = total
    for turn in rounds:
        turn()
    for k in range(nz):
        for place in range(4):
            to_core(place, k).wait_send()
        for made in (first, second, along_x, along_y):
            made(k).wait_send()
        if k < nz - 1:
            along_z(k).wait_send()


def scatter_grads(grads, few, n_dp, n_tensor, collective_id):
    cols = grads.shape[-1]
    rows = grads.shape[1] // n_dp
    nz = n_dp // 2
    small = few is not None
    rounds = bits(n_dp) + bits(n_tensor)
    hbm = pl.BlockSpec(memory_space=pltpu.MemorySpace.HBM)
    vmem = pl.BlockSpec(memory_space=pltpu.MemorySpace.VMEM)
    out_shape = [jax.ShapeDtypeStruct((rows, cols), F32)]
    scratch = [
        pltpu.VMEM((4, nz, rows, cols), BF),
        pltpu.VMEM((4, nz, rows, cols), BF),
        pltpu.VMEM((nz, rows, cols // 2), BF),
        pltpu.VMEM((nz, rows, cols // 2), BF),
        pltpu.VMEM((nz, rows, cols), BF),
        pltpu.VMEM((nz, rows, cols), BF),
        pltpu.VMEM((nz - 1, rows, cols), BF),
        pltpu.SemaphoreType.DMA((4 * nz,)),
        pltpu.SemaphoreType.DMA((9 * nz,)),
        pltpu.SemaphoreType.DMA((9 * nz,)),
    ]
    operands = [grads.reshape(n_tensor, n_dp, rows, cols)]
    if small:
        out_shape.append(jax.ShapeDtypeStruct(few.shape, F32))
        operands.append(few)
        scratch += [
            pltpu.VMEM((rounds,) + few.shape, F32), pltpu.VMEM((rounds,) + few.shape, F32),
            pltpu.SemaphoreType.DMA((rounds,)), pltpu.SemaphoreType.DMA((rounds,)),
        ]
    return pl.pallas_call(
        functools.partial(scatter_kernel, n_dp, n_tensor, small),
        out_shape=out_shape,
        in_specs=[hbm, vmem] if small else [hbm],
        out_specs=[vmem, vmem] if small else [vmem],
        scratch_shapes=scratch,
        compiler_params=params(collective_id=collective_id, has_side_effects=True),
        name="scatter_grads",
    )(*operands)


def window_slots(tokens, rows):
    t = lax.axis_index("tensor")
    count = tokens // BLK
    first = jnp.minimum(t * count * BLK // PACK, rows - 2)
    return [(t * count + j) * BLK // PACK - first for j in range(count)]


def lane_masks(first, count):
    slot = lax.broadcasted_iota(jnp.int32, (1, 256), 1) // HD
    return [(slot == first + i).astype(F32).astype(BF) for i in range(count)]


def stack_heads(block, masks):
    return jnp.concatenate([block * mask for mask in masks], axis=0)


def pick_heads(stacked, masks, size):
    total = None
    for i, mask in enumerate(masks):
        part = stacked[i * size : (i + 1) * size] * mask.astype(F32)
        total = part if total is None else total + part
    return total


def norm_forward(value, gain, shift):
    average = jnp.mean(value, axis=-1, keepdims=True)
    centered = value - average
    variance = jnp.mean(centered * centered, axis=-1, keepdims=True)
    scaled = lax.rsqrt(variance + EPS)
    unit = centered * scaled
    return unit * gain + shift, unit, scaled


def norm_back(grad, unit, scaled, gain):
    inner = grad * gain
    centered = inner - jnp.mean(inner, axis=-1, keepdims=True)
    return scaled * (centered - unit * jnp.mean(inner * unit, axis=-1, keepdims=True))


def attn_fwd_kernel(
    rows, win_ref, own_ref, g_ref, qb_ref, kvb_ref, qseg_ref, kseg_ref, vec_ref,
    q_ref, kv_ref, ctx_ref, mid_ref, unit_ref, rs_ref, acc_ref,
):
    step = pl.program_id(0)
    tokens = own_ref.shape[0]
    heads = 3
    kv_ref[0] = (dot(win_ref[...], g_ref[0, :, 384:768]) + kvb_ref[0]).astype(BF)
    q_ref[0] = (dot(own_ref[...].astype(BF), g_ref[0, :, 0:256]) + qb_ref[0]).astype(BF)
    q_masks, c_masks = lane_masks(0, heads), lane_masks(1, heads)
    for j, slot in enumerate(window_slots(tokens, rows)):
        here = pl.ds(j * BLK, BLK)
        keys = pl.ds(pl.multiple_of(slot * PACK, PACK), PACK)
        stacked = stack_heads(q_ref[0, here, :], q_masks)
        scores = dot_nt(stacked, kv_ref[0, keys, 0:256]) * (HD**-0.5)
        kseg = jnp.where(slot == 0, kseg_ref[0:1], kseg_ref[1:2])
        qseg = qseg_ref[here, :]
        allowed = jnp.logical_and(kseg >= 0, jnp.logical_or(kseg == qseg, qseg < 0))
        allowed = jnp.concatenate([allowed] * heads, axis=0)
        scores = jnp.where(allowed, scores, NEG)
        peak = jnp.max(scores, axis=-1, keepdims=True)
        weights = jnp.exp(scores - peak)
        probs = weights * (1.0 / jnp.sum(weights, axis=-1, keepdims=True))
        out = dot(probs.astype(BF), kv_ref[0, keys, 128:384])
        ctx_ref[0, here, :] = pick_heads(out, c_masks, BLK).astype(BF)
    part = dot_nt(ctx_ref[0], g_ref[0, :, 128:384])

    @pl.when(step == 0)
    def _():
        acc_ref[...] = part

    @pl.when(step > 0)
    def _():
        acc_ref[...] += part

    @pl.when(step == pl.num_programs(0) - 1)
    def _():
        total = own_ref[...].astype(F32) + acc_ref[...] + vec_ref[0:1]
        mid_ref[...], unit_ref[...], rs_ref[...] = norm_forward(total, vec_ref[1:2], vec_ref[2:3])


def attn_fwd(win, own, g, qb, kvb, qseg, kseg, vec, rows):
    n, tokens, dim = g.shape[0], own.shape[0], own.shape[1]
    last = g.shape[2] // dim - 1
    return pl.pallas_call(
        functools.partial(attn_fwd_kernel, rows),
        grid=(n,),
        in_specs=[
            whole(win.shape), whole(own.shape), per_t((1, dim, dim), 0, last),
            per_t((1, 1, 256)), per_t((1, 1, 384)), whole(qseg.shape), whole(kseg.shape), whole(vec.shape),
        ],
        out_specs=[
            per_t((1, tokens, 256)), per_t((1, WIN, 384)), per_t((1, tokens, 256)),
            whole((tokens, dim)), whole((tokens, dim)), whole((tokens, 1)),
        ],
        out_shape=[
            jax.ShapeDtypeStruct((n, tokens, 256), BF), jax.ShapeDtypeStruct((n, WIN, 384), BF),
            jax.ShapeDtypeStruct((n, tokens, 256), BF), jax.ShapeDtypeStruct((tokens, dim), F32),
            jax.ShapeDtypeStruct((tokens, dim), F32), jax.ShapeDtypeStruct((tokens, 1), F32),
        ],
        scratch_shapes=[pltpu.VMEM((tokens, dim), F32)],
        compiler_params=params(),
        name="attn_fwd",
    )(win, own, g, qb, kvb, qseg, kseg, vec)


def ffn_fwd_kernel(
    mid_ref, up_ref, down_ref, ub_ref, vec_ref, act_ref, slope_ref, out_ref, low_ref, unit_ref, rs_ref, acc_ref
):
    step = pl.program_id(0)
    upper = dot(mid_ref[...].astype(BF), up_ref[0]) + ub_ref[0]
    half = 0.5 + 0.5 * lax.erf(upper * (0.5**0.5))
    act_ref[0] = (upper * half).astype(BF)
    slope_ref[0] = (half + upper * (jnp.exp(-0.5 * upper * upper) * 0.3989422804014327)).astype(BF)
    part = dot_nt(act_ref[0], down_ref[0])

    @pl.when(step == 0)
    def _():
        acc_ref[...] = part

    @pl.when(step > 0)
    def _():
        acc_ref[...] += part

    @pl.when(step == pl.num_programs(0) - 1)
    def _():
        total = mid_ref[...] + acc_ref[...] + vec_ref[3:4]
        out, unit_ref[...], rs_ref[...] = norm_forward(total, vec_ref[4:5], vec_ref[5:6])
        out_ref[...] = out
        low_ref[...] = out.astype(BF)


def ffn_fwd(mid, g, ub, vec):
    n, (tokens, dim) = g.shape[0], mid.shape
    return pl.pallas_call(
        ffn_fwd_kernel,
        grid=(n,),
        in_specs=[
            whole(mid.shape), per_t((1, dim, dim), 0, 0), per_t((1, dim, dim), 0, 1), per_t((1, 1, dim)), whole(vec.shape),
        ],
        out_specs=[
            per_t((1, tokens, dim)), per_t((1, tokens, dim)),
            whole((tokens, dim)), whole((tokens, dim)), whole((tokens, dim)), whole((tokens, 1)),
        ],
        out_shape=[
            jax.ShapeDtypeStruct((n, tokens, dim), BF), jax.ShapeDtypeStruct((n, tokens, dim), BF),
            jax.ShapeDtypeStruct((tokens, dim), F32), jax.ShapeDtypeStruct((tokens, dim), BF),
            jax.ShapeDtypeStruct((tokens, dim), F32), jax.ShapeDtypeStruct((tokens, 1), F32),
        ],
        scratch_shapes=[pltpu.VMEM((tokens, dim), F32)],
        compiler_params=params(),
        name="ffn_fwd",
    )(mid, g, g, ub, vec)


def column_sum(value):
    return jnp.sum(value, axis=0, keepdims=True)


def ffn_bwd_kernel(
    grad_ref, mid_ref, unit2_ref, rs2_ref, unit1_ref, rs1_ref, up_ref, down_ref, act_ref, slope_ref, vec_ref,
    dg_ref, ub_ref, dvec_ref, dfirst_ref, acc_ref, low_ref, low_t_ref, mid_t_ref,
):
    step = pl.program_id(0)
    dim = grad_ref.shape[1]

    @pl.when(step == 0)
    def _():
        grad = grad_ref[...]
        dsecond = norm_back(grad, unit2_ref[...], rs2_ref[...], vec_ref[4:5])
        dvec_ref[4:5] = column_sum(grad * unit2_ref[...])
        dvec_ref[5:6] = column_sum(grad)
        dvec_ref[3:4] = column_sum(dsecond)
        dvec_ref[6:8] = jnp.zeros((2, dim), F32)
        acc_ref[...] = dsecond
        low_ref[...] = dsecond.astype(BF)
        low_t_ref[...] = dsecond.T.astype(BF)
        mid_t_ref[...] = mid_ref[...].T.astype(BF)

    dupper = dot(low_ref[...], down_ref[0]) * slope_ref[0].astype(F32)
    ub_ref[0] = column_sum(dupper)
    dupper_low = dupper.astype(BF)
    dg_ref[0, :, 0:dim] = dot(mid_t_ref[...], dupper_low).astype(BF)
    dg_ref[0, :, dim : 2 * dim] = dot(low_t_ref[...], act_ref[0]).astype(BF)
    acc_ref[...] += dot_nt(dupper_low, up_ref[0])

    @pl.when(step == pl.num_programs(0) - 1)
    def _():
        dmid = acc_ref[...]
        dfirst = norm_back(dmid, unit1_ref[...], rs1_ref[...], vec_ref[1:2])
        dvec_ref[1:2] = column_sum(dmid * unit1_ref[...])
        dvec_ref[2:3] = column_sum(dmid)
        dvec_ref[0:1] = column_sum(dfirst)
        dfirst_ref[...] = dfirst


def ffn_bwd(grad, mid, unit2, rs2, unit1, rs1, g, act, slope, vec):
    n, (tokens, dim) = g.shape[0], mid.shape
    full = whole((tokens, dim))
    return pl.pallas_call(
        ffn_bwd_kernel,
        grid=(n,),
        in_specs=[
            full, full, full, whole((tokens, 1)), full, whole((tokens, 1)),
            per_t((1, dim, dim), 0, 0), per_t((1, dim, dim), 0, 1),
            per_t((1, tokens, dim)), per_t((1, tokens, dim)), whole(vec.shape),
        ],
        out_specs=[per_t((1, dim, 2 * dim), 0, 0), per_t((1, 1, dim)), whole((8, dim)), full],
        out_shape=[
            jax.ShapeDtypeStruct(g.shape, BF), jax.ShapeDtypeStruct((n, 1, dim), F32),
            jax.ShapeDtypeStruct((8, dim), F32), jax.ShapeDtypeStruct((tokens, dim), F32),
        ],
        scratch_shapes=[
            pltpu.VMEM((tokens, dim), F32), pltpu.VMEM((tokens, dim), BF),
            pltpu.VMEM((dim, tokens), BF), pltpu.VMEM((dim, tokens), BF),
        ],
        compiler_params=params(),
        name="ffn_bwd",
    )(grad, mid, unit2, rs2, unit1, rs1, g, g, act, slope, vec)


def attn_bwd_kernel(
    rows, dg_in, dfirst_ref, own_ref, win_ref, g_ref, q_ref, kv_ref, ctx_ref, qseg_ref, kseg_ref,
    dg_ref, qb_ref, vb_ref, own_grad_ref, win_grad_ref, low_ref, low_t_ref, own_t_ref, win_t_ref, dctx_ref, dq_ref, dkv_ref,
):
    step = pl.program_id(0)
    tokens = own_ref.shape[0]
    heads = 3

    @pl.when(step == 0)
    def _():
        dfirst = dfirst_ref[...]
        low_ref[...] = dfirst.astype(BF)
        low_t_ref[...] = dfirst.T.astype(BF)
        own_t_ref[...] = own_ref[...].astype(F32).T.astype(BF)
        win_t_ref[...] = win_ref[...].astype(F32).T.astype(BF)
        own_grad_ref[...] = dfirst
        win_grad_ref[...] = jnp.zeros(win_grad_ref.shape, F32)

    dctx_ref[...] = dot(low_ref[...], g_ref[0, :, 128:384]).astype(BF)
    dkv_ref[...] = jnp.zeros(dkv_ref.shape, F32)
    q_masks, c_masks = lane_masks(0, heads), lane_masks(1, heads)
    for j, slot in enumerate(window_slots(tokens, rows)):
        here = pl.ds(j * BLK, BLK)
        keys = pl.ds(pl.multiple_of(slot * PACK, PACK), PACK)
        q_stack = stack_heads(q_ref[0, here, :], q_masks)
        d_stack = stack_heads(dctx_ref[here, :], c_masks)
        scores = dot_nt(kv_ref[0, keys, 0:256], q_stack) * (HD**-0.5)
        kseg = kseg_ref[keys, :]
        qseg = qseg_ref[j : j + 1, :]
        allowed = jnp.logical_and(kseg >= 0, jnp.logical_or(kseg == qseg, qseg < 0))
        allowed = jnp.concatenate([allowed] * heads, axis=1)
        scores = jnp.where(allowed, scores, NEG)
        peak = jnp.max(scores, axis=0, keepdims=True)
        weights = jnp.exp(scores - peak)
        probs = weights * (1.0 / jnp.sum(weights, axis=0, keepdims=True))
        dprobs = dot_nt(kv_ref[0, keys, 128:384], d_stack)
        weighted = probs * dprobs
        inner = jnp.sum(weighted, axis=0, keepdims=True)
        dscores = ((weighted - probs * inner) * (HD**-0.5)).astype(BF)
        dkv_ref[keys, 128:384] += dot(probs.astype(BF), d_stack)
        dkv_ref[keys, 0:256] += dot(dscores, q_stack)
        dq_ref[here, :] = pick_heads(dot_tn(dscores, kv_ref[0, keys, 0:256]), q_masks, BLK)
    dq, dkv = dq_ref[...], dkv_ref[...]
    qb_ref[0] = column_sum(dq)
    vb_ref[0] = column_sum(dkv)
    dq_low, dkv_low = dq.astype(BF), dkv.astype(BF)
    grad_q = dot(own_t_ref[...], dq_low)
    grad_o = dot(low_t_ref[...], ctx_ref[0])
    dg_ref[0, :, 0:128] = grad_q[:, 0:128].astype(BF)
    dg_ref[0, :, 128:256] = (grad_q[:, 128:256] + grad_o[:, 0:128]).astype(BF)
    dg_ref[0, :, 256:384] = grad_o[:, 128:256].astype(BF)
    dg_ref[0, :, 384:768] = dot(win_t_ref[...], dkv_low).astype(BF)
    own_grad_ref[...] += dot_nt(dq_low, g_ref[0, :, 0:256])
    win_grad_ref[...] += dot_nt(dkv_low, g_ref[0, :, 384:768])


def attn_bwd(dg, dfirst, own, win, g, q, kv, ctx, qseg, kseg, rows):
    n, (tokens, dim) = g.shape[0], own.shape
    last = g.shape[2] // dim - 1
    return pl.pallas_call(
        functools.partial(attn_bwd_kernel, rows),
        grid=(n,),
        in_specs=[
            pl.BlockSpec(memory_space=pl.ANY), whole((tokens, dim)), whole((tokens, dim)), whole(win.shape),
            per_t((1, dim, dim), 0, last), per_t((1, tokens, 256)), per_t((1, WIN, 384)), per_t((1, tokens, 256)),
            whole(qseg.shape), whole(kseg.shape),
        ],
        out_specs=[
            per_t((1, dim, dim), 0, last), per_t((1, 1, 256)), per_t((1, 1, 384)),
            whole((tokens, dim)), whole((WIN, dim)),
        ],
        out_shape=[
            jax.ShapeDtypeStruct(dg.shape, BF), jax.ShapeDtypeStruct((n, 1, 256), F32),
            jax.ShapeDtypeStruct((n, 1, 384), F32), jax.ShapeDtypeStruct((tokens, dim), F32),
            jax.ShapeDtypeStruct((WIN, dim), F32),
        ],
        scratch_shapes=[
            pltpu.VMEM((tokens, dim), BF), pltpu.VMEM((dim, tokens), BF), pltpu.VMEM((dim, tokens), BF),
            pltpu.VMEM((dim, WIN), BF), pltpu.VMEM((tokens, 256), BF), pltpu.VMEM((tokens, 256), F32),
            pltpu.VMEM((WIN, 384), F32),
        ],
        input_output_aliases={0: 0},
        compiler_params=params(),
        name="attn_bwd",
    )(dg, dfirst, own, win, g, q, kv, ctx, qseg, kseg)


def body(n_dp, n_tensor, block_input, passage_lengths, qkv_weight, qv_bias, out_weight, out_bias, first_gain,
         first_shift, up_weight, up_bias, down_weight, down_bias, second_gain, second_shift, output_grad):
    layers = qkv_weight.shape[0]
    tokens, dim = block_input.shape
    rows, segments = passage_lengths.shape
    t = lax.axis_index("tensor")
    dp = lax.axis_index("dp")
    shard, units = qkv_weight.shape[2], qkv_weight.shape[3]
    hidden_units = up_weight.shape[2]

    packs = [
        jnp.concatenate(
            [up_weight[l], down_weight[l].T, qkv_weight[l, 0], out_weight[l].T, qkv_weight[l, 1], qkv_weight[l, 2]], axis=1
        )
        for l in range(layers)
    ]
    def biases(small):
        small = small.reshape(n_tensor, n_dp, -1)[..., : layers * each].reshape(n_tensor, n_dp, layers, each)
        qv = small[..., : 2 * piece].reshape(n_tensor, n_dp, layers, 2, piece).transpose(2, 3, 0, 1, 4)
        qv = qv.reshape(layers, 2, n_tensor, 1, units)
        q_bias = jnp.pad(qv[:, 0], ((0, 0), (0, 0), (0, 0), (0, 256 - units)))
        kv_bias = jnp.pad(qv[:, 1], ((0, 0), (0, 0), (0, 0), (units, 0)))
        return q_bias, kv_bias, small[..., 2 * piece :].transpose(2, 0, 1, 3).reshape(layers, n_tensor, 1, hidden_units)

    piece, wide = qv_bias.shape[2], up_bias.shape[1]
    each = 2 * piece + wide
    few = jnp.concatenate([qv_bias.reshape(layers, -1), up_bias], axis=1).astype(F32).reshape(-1)
    few = jnp.pad(few, (0, -few.shape[0] % 1024)).reshape(-1, 128)

    zero = jnp.zeros((1, dim), F32)
    vecs = [
        jnp.concatenate(
            [v[l : l + 1] for v in (out_bias, first_gain, first_shift, down_bias, second_gain, second_shift)] + [zero, zero],
            axis=0,
        )
        for l in range(layers)
    ]

    ends = jnp.cumsum(passage_lengths, axis=1, dtype=jnp.int32)
    places = jnp.arange(PACK, dtype=jnp.int32)
    seg = jnp.sum((places[None, :, None] >= ends[:, None, :]).astype(jnp.int32), axis=2, dtype=jnp.int32)
    seg = jnp.where(seg == segments, -1, seg)
    first_row = jnp.minimum(t * tokens // PACK, rows - 2)
    kseg = lax.dynamic_slice(seg, (first_row, 0), (2, PACK))
    kcol = kseg.reshape(WIN, 1)
    qseg = lax.dynamic_slice(seg.reshape(-1), (t * tokens,), (tokens,))
    qcol = qseg.reshape(tokens, 1)
    qrow = qseg.reshape(tokens // BLK, BLK)

    pad = PACK // 2
    start = pad + first_row * PACK - (t - 1) * tokens
    up = [(i, i + 1) for i in range(n_tensor - 1)]
    down = [(i + 1, i) for i in range(n_tensor - 1)]
    edge = jnp.zeros((pad, dim), BF)

    def window(low):
        before = lax.ppermute(low, "tensor", up)
        after = lax.ppermute(low, "tensor", down)
        line = jnp.concatenate([edge, before, low, after, edge], axis=0)
        return lax.dynamic_slice(line, (start, 0), (WIN, dim))

    def window_back(own_grad, win_grad):
        line = lax.dynamic_update_slice(jnp.zeros((2 * pad + 3 * tokens, dim), F32), win_grad, (start, 0))
        before = lax.ppermute(line[pad : pad + tokens].astype(BF), "tensor", down)
        after = lax.ppermute(line[pad + 2 * tokens : pad + 3 * tokens].astype(BF), "tensor", up)
        return own_grad + line[pad + tokens : pad + 2 * tokens] + before.astype(F32) + after.astype(F32)

    own, win = block_input, window(block_input)
    kept = []
    for l in range(layers):
        if l == 0:
            g, small = gather_weights(packs[l], few, n_dp, n_tensor, 0)
            q_bias, kv_bias, u_bias = biases(small)
        else:
            (g,) = gather_weights(packs[l], None, n_dp, n_tensor, 2)
        q, kv, ctx, mid, unit1, rs1 = attn_fwd(win, own, g, q_bias[l], kv_bias[l], qcol, kseg, vecs[l], rows)
        act, slope, out, low, unit2, rs2 = ffn_fwd(mid, g, u_bias[l], vecs[l])
        kept.append((own, win, g, q, kv, ctx, mid, unit1, rs1, act, slope, unit2, rs2))
        own = out
        if l < layers - 1:
            win = window(low)
    block_output = own

    grad = output_grad
    pieces, smalls = [None] * layers, [None] * layers
    for l in reversed(range(layers)):
        own, win, g, q, kv, ctx, mid, unit1, rs1, act, slope, unit2, rs2 = kept[l]
        dg, ub, dvec, dfirst = ffn_bwd(grad, mid, unit2, rs2, unit1, rs1, g, act, slope, vecs[l])
        dg, qb, vb, own_grad, win_grad = attn_bwd(dg, dfirst, own, win, g, q, kv, ctx, qrow, kcol, rows)
        grad = window_back(own_grad, win_grad)
        smalls[l] = jnp.concatenate(
            [dvec[:6].reshape(-1), qb[:, 0, :units].reshape(-1), vb[:, 0, units:].reshape(-1), ub.reshape(-1)]
        )
        if l == 0:
            few = jnp.stack(smalls)
            size = few.shape
            pieces[l], totals = scatter_grads(dg, few.reshape(-1, 128), n_dp, n_tensor, 1)
            totals = totals.reshape(size)
        else:
            (pieces[l],) = scatter_grads(dg, None, n_dp, n_tensor, 3)
    vec_totals = totals[:, : 6 * dim].reshape(layers, 6, dim)
    qv_totals = totals[:, 6 * dim : 6 * dim + 2 * n_tensor * units].reshape(layers, 2, n_tensor * units)
    u_totals = totals[:, 6 * dim + 2 * n_tensor * units :]
    qv_grad = lax.dynamic_slice(qv_totals, (0, 0, (t * n_dp + dp) * piece), (layers, 2, piece))
    u_grad = lax.dynamic_slice(u_totals, (0, (t * n_dp + dp) * wide), (layers, wide))

    both = jnp.stack(pieces)
    base = 2 * hidden_units
    cols = [both[:, :, base + i * units : base + (i + 1) * units] for i in range(4)]
    return (
        block_output,
        grad,
        jnp.stack([cols[0], cols[2], cols[3]], axis=1),
        qv_grad,
        cols[1].transpose(0, 2, 1),
        vec_totals[:, 0],
        vec_totals[:, 1],
        vec_totals[:, 2],
        both[:, :, :hidden_units],
        u_grad,
        both[:, :, hidden_units:base].transpose(0, 2, 1),
        vec_totals[:, 3],
        vec_totals[:, 4],
        vec_totals[:, 5],
    )


def solution(mesh):
    n_dp, n_tensor = mesh.shape["dp"], mesh.shape["tensor"]
    tokens = P(("dp", "tensor"), None)
    in_specs = (
        tokens, P("dp", None), P(None, None, "dp", "tensor"), P(None, None, ("tensor", "dp")), P(None, "tensor", "dp"),
        P(), P(), P(), P(None, "dp", "tensor"), P(None, ("tensor", "dp")), P(None, "tensor", "dp"), P(), P(), P(), tokens,
    )
    out_specs = (
        tokens, tokens, P(None, None, "dp", "tensor"), P(None, None, ("tensor", "dp")), P(None, "tensor", "dp"),
        P(), P(), P(), P(None, "dp", "tensor"), P(None, ("tensor", "dp")), P(None, "tensor", "dp"), P(), P(), P(),
    )
    return jax.shard_map(
        functools.partial(body, n_dp, n_tensor), mesh=mesh, in_specs=in_specs, out_specs=out_specs, check_vma=False
    )
```

```python
import functools

import jax
import jax.numpy as jnp
from jax import lax
from jax.experimental import pallas as pl
from jax.experimental.pallas import tpu as pltpu
from jax.sharding import PartitionSpec as P

HD = 64
PACK = 512
BLK = 128
PER = PACK // BLK
WIN = 2 * PACK
EPS = 1e-05
NEG = -1e30
MESH = pl.DeviceIdType.MESH
BF = jnp.bfloat16
F32 = jnp.float32
I32 = jnp.int32
HBM = pl.BlockSpec(memory_space=pltpu.MemorySpace.HBM)
VMEM = pl.BlockSpec(memory_space=pltpu.MemorySpace.VMEM)
SMEM = pl.BlockSpec(memory_space=pltpu.MemorySpace.SMEM)
Q_AT, KV_AT, U_AT = 0, 256, 640


def dot(a, b):
    return jnp.dot(a, b, preferred_element_type=F32)


def dot_nt(a, b):
    return lax.dot_general(a, b, (((1,), (1,)), ((), ())), preferred_element_type=F32)


def dot_tn(a, b):
    return lax.dot_general(a, b, (((0,), (0,)), ((), ())), preferred_element_type=F32)


def whole(shape):
    return pl.BlockSpec(shape, lambda t: (0,) * len(shape))


def per_t(shape, *rest):
    tail = rest if rest else (0,) * (len(shape) - 1)
    return pl.BlockSpec(shape, lambda t: (t,) + tail)


def sds(shape, dtype=F32):
    return jax.ShapeDtypeStruct(shape, dtype)


def column_sum(value):
    return jnp.sum(value, axis=0, keepdims=True)


def flip(value):
    return value.astype(F32).T.astype(BF)


class Place:
    def __init__(self, n_dp, n_tensor):
        self.n_dp, self.n_tensor = n_dp, n_tensor
        self.nz = n_dp // 2
        dp, tensor = lax.axis_index("dp"), lax.axis_index("tensor")
        self.dp, self.tensor = dp, tensor
        self.z, self.y = dp // 2, dp % 2
        self.x, self.c = tensor // 2, tensor % 2
        self.dp_y = 2 * self.z + 1 - self.y
        self.t_x = 2 * (1 - self.x) + self.c
        self.t_c = 2 * self.x + 1 - self.c
        self.t_xc = 2 * (1 - self.x) + 1 - self.c
        self.to_x = (dp, self.t_x)
        self.to_y = (self.dp_y, tensor)
        self.to_c = (dp, self.t_c)

    def d(self, z, same_y=True):
        return 2 * z + (self.y if same_y else 1 - self.y)

    def near(self):
        return [(self.to_x, None), (self.to_y, None), (self.to_c, None)]

    def along_z(self):
        return [((self.dp - 2, self.tensor), self.z > 0), ((self.dp + 2, self.tensor), self.z < self.nz - 1)]

    def far_z(self):
        return [((self.dp ^ (2 << b), self.tensor), None) for b in range(1, bits(self.nz))]

    def beside(self):
        other = self.tensor - 1 + 2 * self.c
        return [((self.dp, other), jnp.logical_and(other >= 0, other < self.n_tensor))]


def meet(peers):
    barrier = pltpu.get_barrier_semaphore()
    count = 0
    for device, valid in peers:
        def signal(device=device):
            pl.semaphore_signal(barrier, inc=1, device_id=device, device_id_type=MESH)
        if valid is None:
            signal()
            count = count + 1
        else:
            pl.when(valid)(signal)
            count = count + valid.astype(I32)
    pl.semaphore_wait(barrier, count)


def bits(n):
    return n.bit_length() - 1


def pairs(me):
    found = [(me.dp, me.tensor ^ (1 << b)) for b in range(bits(me.n_tensor))]
    return found + [(me.dp ^ (1 << b), me.tensor) for b in range(bits(me.n_dp))]


def rounds_of(n_dp, n_tensor):
    return bits(n_dp) + bits(n_tensor)


def doubling_sum(me, first, total_ref, part_ref, come_ref, send_sem, recv_sem):
    copies = [
        pltpu.make_async_remote_copy(
            src_ref=part_ref.at[i], dst_ref=come_ref.at[i], send_sem=send_sem.at[i], recv_sem=recv_sem.at[i],
            device_id=device, device_id_type=MESH,
        )
        for i, device in enumerate(pairs(me))
    ]

    def begin():
        first()
        copies[0].start()

    def middle(i):
        copies[i].wait_recv()
        total = part_ref[i] + come_ref[i]
        if i + 1 < len(copies):
            part_ref[i + 1] = total
            copies[i + 1].start()
        else:
            total_ref[...] = total

    def end():
        for copy in copies:
            copy.wait_send()

    return [begin] + [functools.partial(middle, i) for i in range(len(copies))] + [end]


def doubling_scratch(shape, n_dp, n_tensor):
    n = rounds_of(n_dp, n_tensor)
    return [
        pltpu.VMEM((n,) + shape, F32), pltpu.VMEM((n,) + shape, F32),
        pltpu.SemaphoreType.DMA((n,)), pltpu.SemaphoreType.DMA((n,)),
    ]


class Window:
    def __init__(self, me, tokens, rows):
        self.me, self.count, self.rows = me, tokens // BLK, rows

    def first(self, t):
        return jnp.minimum(t * self.count // PER, self.rows - 2)

    def blocks(self):
        t = self.me.tensor
        found = []
        for j in range(self.count):
            g = t * self.count + j
            found.append((g // PER, g // PER - self.first(t), g % PER))
        return found

    def needed(self, source, j, target):
        g = source * self.count + j
        row = g // PER
        inside = jnp.logical_and(row >= target * self.count // PER, row <= (target * self.count + self.count - 1) // PER)
        exists = jnp.logical_and(jnp.logical_and(source >= 0, source < self.me.n_tensor),
                                 jnp.logical_and(target >= 0, target < self.me.n_tensor))
        return jnp.logical_and(inside, exists), g - self.first(target) * PER

    def own_places(self):
        t = self.me.tensor
        return [t * self.count + j - self.first(t) * PER for j in range(self.count)]

    def _each(self, outgoing):
        t = self.me.tensor
        for i, step in enumerate((1, -1)):
            for j in range(self.count):
                source, target = (t, t + step) if outgoing else (t - step, t)
                valid, place = self.needed(source, j, target)
                yield i * self.count + j, j, source, target, valid, pl.multiple_of(place * BLK, BLK)

    def _copy(self, source, target, slot, device, sems):
        return pltpu.make_async_remote_copy(
            src_ref=source, dst_ref=target, send_sem=sems[0].at[slot], recv_sem=sems[1].at[slot],
            device_id=(self.me.dp, device), device_id_type=MESH,
        )

    def send(self, low_ref, win_ref, sems, what="start"):
        for slot, j, source, target, valid, place in self._each(True):
            copy = self._copy(low_ref.at[pl.ds(j * BLK, BLK)], win_ref.at[pl.ds(place, BLK)], slot, target, sems)
            pl.when(valid)(getattr(copy, what))

    def receive(self, win_ref, sems):
        for slot, j, source, target, valid, place in self._each(False):
            here = win_ref.at[pl.ds(place, BLK)]
            pl.when(valid)(pltpu.make_async_copy(here, here, sems[1].at[slot]).wait)

    def send_back(self, grad_ref, back_ref, sems, what="start"):
        for slot, j, source, target, valid, place in self._each(False):
            copy = self._copy(grad_ref.at[pl.ds(place, BLK)], back_ref.at[slot], slot, source, sems)
            pl.when(valid)(getattr(copy, what))

    def receive_back(self, back_ref, sems, add):
        for slot, j, source, target, valid, place in self._each(True):
            def take(slot=slot, j=j):
                pltpu.make_async_copy(back_ref.at[slot], back_ref.at[slot], sems[1].at[slot]).wait()
                add(j, back_ref[slot])
            pl.when(valid)(take)

    def sems(tokens):
        n = 2 * (tokens // BLK)
        return [pltpu.SemaphoreType.DMA((n,)), pltpu.SemaphoreType.DMA((n,))]


class Gather:
    def __init__(self, own, n_dp, n_tensor):
        rows, cols = own.shape
        slots = 12 * (n_dp // 2)
        self.operands, self.in_specs = [own], [HBM]
        self.out_shape, self.out_specs = [sds((n_tensor, n_dp, rows, cols), own.dtype)], [HBM]
        self.scratch = [pltpu.SemaphoreType.DMA, pltpu.SemaphoreType.DMA((slots,)), pltpu.SemaphoreType.DMA((slots,))]

    def peers(self, me):
        return me.near() + me.along_z()

    def rounds(self, me, own_ref, out_ref, own_sem, send_sem, recv_sem):
        nz, cols = me.nz, own_ref.shape[-1]
        sixth = cols // 6 // 128 * 128
        cuts = {None: (0, cols), 0: (0, cols // 2), 1: (cols // 2, cols), 2: (0, sixth), 3: (sixth, 2 * sixth), 4: (2 * sixth, cols)}

        def piece(t, d, part):
            lo, hi = cuts[part]
            return out_ref.at[t, d] if part is None else out_ref.at[t, d, :, pl.ds(lo, hi - lo)]

        def copy(source, t, d, part, route, p, device):
            slot = route * nz + p
            return pltpu.make_async_remote_copy(
                src_ref=source if source is not None else piece(t, d, part), dst_ref=piece(t, d, part),
                send_sem=send_sem.at[slot], recv_sem=recv_sem.at[slot], device_id=device, device_id_type=MESH,
            )

        def arrived(t, d, part, route, p):
            pltpu.make_async_copy(piece(t, d, part), piece(t, d, part), recv_sem.at[route * nz + p]).wait()

        mine = pltpu.make_async_copy(own_ref, out_ref.at[me.tensor, me.dp], own_sem)
        up, down = (me.dp + 2, me.tensor), (me.dp - 2, me.tensor)
        can_up, can_down = me.z < nz - 1, me.z > 0

        def z_copy(p, upward, source=None):
            return copy(source, me.tensor, me.d(p), None, 0 if upward else 1, p, up if upward else down)

        def x_copy(p, source=None):
            return copy(source, me.tensor, me.d(p), None, 2, p, me.to_x)

        def y_copy(p, source=None):
            return copy(source, me.tensor, me.d(p), None, 3, p, me.to_y)

        def first_copy(p, here):
            return copy(None, me.t_x, me.d(p), 0 if here else 2, 4, p, me.to_y)

        def second_copy(p, here):
            return copy(None, me.tensor, me.d(p, False), 1 if here else 3, 5, p, me.to_x)

        def diagonal_z(p, upward):
            return copy(None, me.t_x, me.d(p, False), 4, 6 if upward else 7, p, up if upward else down)

        def core_copy(kind, p, source=None):
            return copy(source, me.tensor if kind in (0, 2) else me.t_x, me.d(p, kind in (0, 1)), None, 8 + kind, p, me.to_c)

        def own_round():
            mine.start()
            pl.when(can_up)(z_copy(me.z, True, own_ref).start)
            pl.when(can_down)(z_copy(me.z, False, own_ref).start)
            x_copy(me.z, own_ref).start()
            y_copy(me.z, own_ref).start()
            core_copy(0, me.z, own_ref).start()

        def z_round(p, upward, valid):
            @pl.when(valid)
            def _():
                arrived(me.tensor, me.d(p), None, 0 if upward else 1, p)
                pl.when(can_up if upward else can_down)(z_copy(p, upward).start)
                x_copy(p).start()
                y_copy(p).start()
                core_copy(0, p).start()

        def xy_round(p, here, valid=None):
            def go():
                arrived(me.t_x, me.d(p), None, 2, p)
                first_copy(p, here).start()
                core_copy(1, p).start()
                arrived(me.tensor, me.d(p, False), None, 3, p)
                second_copy(p, here).start()
                core_copy(2, p).start()
            go() if valid is None else pl.when(valid)(go)

        def diagonal_here():
            arrived(me.t_x, me.d(me.z, False), 0, 4, me.z)
            arrived(me.t_x, me.d(me.z, False), 1, 5, me.z)
            pl.when(can_up)(diagonal_z(me.z, True).start)
            pl.when(can_down)(diagonal_z(me.z, False).start)
            core_copy(3, me.z).start()

        def diagonal_round(p, upward, valid):
            @pl.when(valid)
            def _():
                arrived(me.t_x, me.d(p, False), 4, 6 if upward else 7, p)
                pl.when(can_up if upward else can_down)(diagonal_z(p, upward).start)
                arrived(me.t_x, me.d(p, False), 2, 4, p)
                arrived(me.t_x, me.d(p, False), 3, 5, p)
                core_copy(3, p).start()

        def middle(s):
            low, high = me.z - s, me.z + s
            if s < nz:
                z_round(low, True, low >= 0)
                z_round(high, False, high < nz)
            if s == 1:
                xy_round(me.z, True)
            elif s - 1 < nz:
                xy_round(low + 1, False, low + 1 >= 0)
                xy_round(high - 1, False, high - 1 < nz)
            if s == 2:
                diagonal_here()
            elif 2 < s < nz + 2:
                diagonal_round(low + 2, True, low + 2 >= 0)
                diagonal_round(high - 2, False, high - 2 < nz)

        def end():
            for p in range(nz):
                for kind in range(4):
                    arrived(me.t_c if kind in (0, 2) else me.t_xc, me.d(p, kind in (0, 1)), None, 8 + kind, p)
            mine.wait()
            for p in range(nz):
                here = me.z == p
                pl.when(jnp.logical_and(can_up, p <= me.z))(z_copy(p, True).wait_send)
                pl.when(jnp.logical_and(can_down, p >= me.z))(z_copy(p, False).wait_send)
                x_copy(p).wait_send()
                y_copy(p).wait_send()
                for made in (first_copy, second_copy):
                    pl.when(here)(made(p, True).wait_send)
                    pl.when(jnp.logical_not(here))(made(p, False).wait_send)
                pl.when(jnp.logical_and(can_up, p <= me.z))(diagonal_z(p, True).wait_send)
                pl.when(jnp.logical_and(can_down, p >= me.z))(diagonal_z(p, False).wait_send)
                for kind in range(4):
                    core_copy(kind, p).wait_send()

        return [own_round] + [functools.partial(middle, s) for s in range(1, nz + 2)] + [end]


class Scatter:
    def __init__(self, grads, n_dp, n_tensor):
        rows, cols = grads.shape[1] // n_dp, grads.shape[2]
        nz = n_dp // 2
        self.operands, self.in_specs = [grads.reshape(n_tensor, n_dp, rows, cols)], [HBM]
        self.out_shape, self.out_specs = [sds((rows, cols))], [pl.BlockSpec((rows, cols), lambda *_: (0, 0))]
        self.scratch = [
            pltpu.VMEM((4, nz, rows, cols), BF),
            pltpu.VMEM((4, nz, rows, cols), BF),
            pltpu.VMEM((nz, rows, cols // 2), BF),
            pltpu.VMEM((nz, rows, cols // 2), BF),
            pltpu.VMEM((nz, rows, cols), BF),
            pltpu.VMEM((nz, rows, cols), BF),
            pltpu.VMEM((nz - 1, rows, cols), BF),
            pltpu.SemaphoreType.DMA((4 * nz,)),
            pltpu.SemaphoreType.DMA((9 * nz,)),
            pltpu.SemaphoreType.DMA((9 * nz,)),
        ]

    def order(self, me):
        return [lax.rem(me.z + k, me.nz) for k in range(1, me.nz)] + [me.z]

    def peers(self, me):
        return me.near() + [((me.d(z), me.tensor), None) for z in self.order(me)[:-1]]

    def rounds(
        self, me, g_ref, out_ref, mine, core_in, first_in, second_in, x_in, y_in, z_in, load_sem, send_sem, recv_sem
    ):
        nz = me.nz
        half = g_ref.shape[-1] // 2
        zs = self.order(me)

        def owner(place, k):
            return place in (0, 1), me.d(zs[k], place not in (0, 2))

        def remote(source, target, slot, device):
            return pltpu.make_async_remote_copy(
                src_ref=source, dst_ref=target, send_sem=send_sem.at[slot], recv_sem=recv_sem.at[slot],
                device_id=device, device_id_type=MESH,
            )

        def to_core(place, k):
            x_other, d = owner(place, k)
            return remote(g_ref.at[me.t_xc if x_other else me.t_c, d], core_in.at[place, k], place * nz + k, me.to_c)

        def load(place, k):
            x_other, d = owner(place, k)
            return pltpu.make_async_copy(
                g_ref.at[me.t_x if x_other else me.tensor, d], mine.at[place, k], load_sem.at[place * nz + k]
            )

        def first(k):
            return remote(mine.at[0, k, :, pl.ds(0, half)], first_in.at[k], 4 * nz + k, me.to_x)

        def second(k):
            return remote(mine.at[0, k, :, pl.ds(half, half)], second_in.at[k], 5 * nz + k, me.to_y)

        def along_x(k):
            return remote(mine.at[1, k], x_in.at[k], 6 * nz + k, me.to_x)

        def along_y(k):
            return remote(mine.at[2, k], y_in.at[k], 7 * nz + k, me.to_y)

        def along_z(k):
            return remote(mine.at[3, k], z_in.at[k], 8 * nz + k, (me.d(zs[k]), me.tensor))

        def both(place, k):
            load(place, k).wait()
            to_core(place, k).wait_recv()
            return mine[place, k].astype(F32) + core_in[place, k].astype(F32)

        def begin():
            for k in range(nz):
                for place in range(4):
                    to_core(place, k).start()
                    load(place, k).start()

        def middle(step):
            if step < nz:
                k = step
                mine[0, k] = both(0, k).astype(BF)
                first(k).start()
                second(k).start()
            if 0 <= step - 1 < nz:
                k = step - 1
                total = both(1, k)
                second(k).wait_recv()
                mine[1, k, :, :half] = total[:, :half].astype(BF)
                mine[1, k, :, half:] = (total[:, half:] + second_in[k].astype(F32)).astype(BF)
                along_x(k).start()
                total = both(2, k)
                first(k).wait_recv()
                mine[2, k, :, half:] = total[:, half:].astype(BF)
                mine[2, k, :, :half] = (total[:, :half] + first_in[k].astype(F32)).astype(BF)
                along_y(k).start()
            if 0 <= step - 2 < nz:
                k = step - 2
                total = both(3, k)
                along_x(k).wait_recv()
                total += x_in[k].astype(F32)
                along_y(k).wait_recv()
                total += y_in[k].astype(F32)
                if k < nz - 1:
                    mine[3, k] = total.astype(BF)
                    along_z(k).start()
                else:
                    for j in range(nz - 1):
                        along_z(j).wait_recv()
                        total += z_in[j].astype(F32)
                    out_ref[...] = total

        def end():
            for k in range(nz):
                for place in range(4):
                    to_core(place, k).wait_send()
                for made in (first, second, along_x, along_y):
                    made(k).wait_send()
                if k < nz - 1:
                    along_z(k).wait_send()

        return [begin] + [functools.partial(middle, step) for step in range(nz + 2)] + [end]


class Still:
    operands, in_specs, out_shape, out_specs, scratch = [], [], [], [], []


def call(kernel, name, side, mesh_sizes, collective_id, operands, in_specs, out_shape, out_specs, scratch, early=1):
    n = mesh_sizes[1]
    n_in, n_out, n_scr = len(operands), len(out_shape), len(scratch)
    m_in, m_out = len(side.operands), len(side.out_shape)

    def body(*refs):
        me = Place(*mesh_sizes)
        cut, parts = 0, []
        for size in (n_in, m_in, n_out, m_out, n_scr):
            parts.append(refs[cut : cut + size])
            cut += size
        parts.append(refs[cut:])
        rounds = []
        if not isinstance(side, Still):
            rounds = side.rounds(me, *parts[1], *parts[3], *parts[5])
        step = pl.program_id(0)

        def before(peers=()):
            if not rounds:
                return
            for i in range(n):
                @pl.when(step == i)
                def _(i=i):
                    if i == 0:
                        meet(side.peers(me) + list(peers))
                        for turn in rounds[:early]:
                            turn()
                    else:
                        rounds[early + i - 1]()

        def after():
            for turn in rounds[early + n - 1 :]:
                turn()

        kernel(me, before, after, *parts[0], *parts[2], *parts[4])

    remote = {} if isinstance(side, Still) else dict(collective_id=collective_id, has_side_effects=True)
    return pl.pallas_call(
        body, grid=(n,), in_specs=in_specs + side.in_specs, out_specs=out_specs + side.out_specs,
        out_shape=out_shape + side.out_shape, scratch_shapes=scratch + side.scratch,
        compiler_params=pltpu.CompilerParams(vmem_limit_bytes=60 * 1024 * 1024, **remote), name=name,
    )(*operands, *side.operands)


def start_kernel(
    n_dp, n_tensor, gather, rows,
    qkv_ref, ow_ref, up_ref, down_ref, qvb_ref, ub_ref, own_ref,
    a1_ref, f0_ref, f1_ref, win_ref, bias_ref, ga_ref,
    a0_ref, part_ref, come_ref, few_send, few_recv, win_send, win_recv, *gather_sems,
):
    me = Place(n_dp, n_tensor)
    layers = qkv_ref.shape[0]
    window = Window(me, own_ref.shape[0], rows)

    def pack_a(l, target):
        units = qkv_ref.shape[3]
        target[:, 0:units] = qkv_ref[l, 0]
        target[:, units : 2 * units] = flip(ow_ref[l])
        target[:, 2 * units : 3 * units] = qkv_ref[l, 1]
        target[:, 3 * units : 4 * units] = qkv_ref[l, 2]

    def pack_f(l, target):
        units = up_ref.shape[2]
        target[:, 0:units] = up_ref[l]
        target[:, units : 2 * units] = flip(down_ref[l])

    def place_biases():
        piece, wide = qvb_ref.shape[2], ub_ref.shape[1]
        units = qkv_ref.shape[3]
        width = bias_ref.shape[1]

        def spread(values, start):
            size = values.shape[1]
            source = lax.broadcasted_iota(I32, (size, width), 0)
            target = lax.broadcasted_iota(I32, (size, width), 1)
            return dot(values, (target == source + start).astype(F32).astype(BF))

        u = spread(ub_ref[...], U_AT + me.dp * wide)
        line = lax.broadcasted_iota(I32, (layers * n_tensor, width), 0)
        total = jnp.zeros((layers * n_tensor, width), F32)
        for l in range(layers):
            row = u[l : l + 1]
            row += spread(qvb_ref[l], Q_AT + me.dp * piece)[0:1]
            row += spread(qvb_ref[l], KV_AT + units + me.dp * piece)[1:2]
            total += jnp.where(line == l * n_tensor + me.tensor, row, 0.0)
        part_ref[0] = total

    pack_a(0, a0_ref)
    win_ref[...] = jnp.zeros(win_ref.shape, BF)
    meet(gather.peers(me) + me.far_z() + me.beside())
    turns = gather.rounds(me, a0_ref, ga_ref, *gather_sems)
    few = doubling_sum(me, place_biases, bias_ref, part_ref, come_ref, few_send, few_recv)
    turns[0]()
    window.send(own_ref, win_ref, (win_send, win_recv))
    few[0]()
    for j, place in enumerate(window.own_places()):
        win_ref[pl.ds(pl.multiple_of(place * BLK, BLK), BLK), :] = own_ref[pl.ds(j * BLK, BLK), :]
    turns[1]()
    few[1]()
    pack_f(0, f0_ref)
    turns[2]()
    few[2]()
    pack_a(1, a1_ref)
    turns[3]()
    few[3]()
    pack_f(1, f1_ref)
    rest, more = turns[4:], few[4:]
    for i in range(max(len(rest), len(more))):
        if i < len(rest):
            rest[i]()
        if i < len(more):
            more[i]()
    window.receive(win_ref, (win_send, win_recv))
    window.send(own_ref, win_ref, (win_send, win_recv), "wait_send")


def start(qkv, ow, up, down, qvb, ub, own, rows, n_dp, n_tensor):
    layers, _, shard, units = qkv.shape
    tokens, dim = own.shape
    a_shape, f_shape = (shard, 4 * units), (shard, 2 * up.shape[2])
    width = U_AT + up.shape[2]
    gather = Gather(sds(a_shape, BF), n_dp, n_tensor)
    few = (layers * n_tensor, width)
    return pl.pallas_call(
        functools.partial(start_kernel, n_dp, n_tensor, gather, rows),
        in_specs=[VMEM] * 7,
        out_specs=[VMEM] * 5 + [HBM],
        out_shape=[sds(a_shape, BF), sds(f_shape, BF), sds(f_shape, BF), sds((WIN, dim), BF), sds(few)] + gather.out_shape,
        scratch_shapes=[pltpu.VMEM(a_shape, BF)] + doubling_scratch(few, n_dp, n_tensor) + Window.sems(tokens) + gather.scratch,
        compiler_params=pltpu.CompilerParams(vmem_limit_bytes=40 * 1024 * 1024, collective_id=0, has_side_effects=True),
        name="start",
    )(qkv, ow, up, down, qvb, ub, own)


def ends_of(len_ref, row):
    total, ends = 0, []
    for k in range(len_ref.shape[1]):
        total = total + len_ref[row, k]
        ends.append(total)
    return ends


def segments(ends, place):
    seg = jnp.zeros(place.shape, I32)
    for end in ends:
        seg += (place >= end).astype(I32)
    return jnp.where(seg == len(ends), -1, seg)


def allowed_of(len_ref, row, offset, key_axis, heads):
    ends = ends_of(len_ref, row)
    k_shape = (1, PACK) if key_axis == 1 else (PACK, 1)
    q_shape = (BLK, 1) if key_axis == 1 else (1, BLK)
    kseg = segments(ends, lax.broadcasted_iota(I32, k_shape, key_axis))
    qseg = segments(ends, lax.broadcasted_iota(I32, q_shape, 1 - key_axis) + offset)
    allowed = jnp.logical_and(kseg >= 0, jnp.logical_or(kseg == qseg, qseg < 0))
    return jnp.concatenate([allowed] * heads, axis=1 - key_axis)


def lane_masks(first, count):
    slot = lax.broadcasted_iota(jnp.int32, (1, 256), 1) // HD
    return [(slot == first + i).astype(F32).astype(BF) for i in range(count)]


def stack_heads(block, masks):
    return jnp.concatenate([block * mask for mask in masks], axis=0)


def pick_heads(stacked, masks, size):
    total = None
    for i, mask in enumerate(masks):
        part = stacked[i * size : (i + 1) * size] * mask.astype(F32)
        total = part if total is None else total + part
    return total


def norm_forward(value, gain, shift):
    average = jnp.mean(value, axis=-1, keepdims=True)
    centered = value - average
    variance = jnp.mean(centered * centered, axis=-1, keepdims=True)
    scaled = lax.rsqrt(variance + EPS)
    unit = centered * scaled
    return unit * gain + shift, unit, scaled


def norm_back(grad, unit, scaled, gain):
    inner = grad * gain
    centered = inner - jnp.mean(inner, axis=-1, keepdims=True)
    return scaled * (centered - unit * jnp.mean(inner * unit, axis=-1, keepdims=True))


def attn_fwd_kernel(
    rows, layer, me, before, after, len_ref, win_ref, own_ref, g_ref, bias_ref, ob_ref, gain_ref, shift_ref,
    q_ref, kv_ref, ctx_ref, mid_ref, unit_ref, rs_ref, acc_ref,
):
    step, n = pl.program_id(0), pl.num_programs(0)
    tokens = own_ref.shape[0]
    heads = 3
    before()
    line = pl.ds(layer * me.n_tensor + step, 1)
    kv_ref[0] = (dot(win_ref[...], g_ref[0, :, 384:768]) + bias_ref[line, KV_AT : KV_AT + 384]).astype(BF)
    q_ref[0] = (dot(own_ref[...].astype(BF), g_ref[0, :, 0:256]) + bias_ref[line, Q_AT : Q_AT + 256]).astype(BF)
    q_masks, c_masks = lane_masks(0, heads), lane_masks(1, heads)
    for j, (row, slot, part) in enumerate(Window(me, tokens, rows).blocks()):
        here = pl.ds(j * BLK, BLK)
        keys = pl.ds(pl.multiple_of(slot * PACK, PACK), PACK)
        stacked = stack_heads(q_ref[0, here, :], q_masks)
        scores = dot_nt(stacked, kv_ref[0, keys, 0:256]) * (HD**-0.5)
        scores = jnp.where(allowed_of(len_ref, row, part * BLK, 1, heads), scores, NEG)
        peak = jnp.max(scores, axis=-1, keepdims=True)
        weights = jnp.exp(scores - peak)
        probs = weights * (1.0 / jnp.sum(weights, axis=-1, keepdims=True))
        out = dot(probs.astype(BF), kv_ref[0, keys, 128:384])
        ctx_ref[0, here, :] = pick_heads(out, c_masks, BLK).astype(BF)
    part = dot_nt(ctx_ref[0], g_ref[0, :, 128:384])

    @pl.when(step == 0)
    def _():
        acc_ref[...] = part

    @pl.when(step > 0)
    def _():
        acc_ref[...] += part

    @pl.when(step == n - 1)
    def _():
        line = pl.ds(layer, 1)
        total = own_ref[...].astype(F32) + acc_ref[...] + ob_ref[line, :]
        mid_ref[...], unit_ref[...], rs_ref[...] = norm_forward(total, gain_ref[line, :], shift_ref[line, :])
        after()


def attn_fwd(side, cid, layer, sizes, lens, win, own, g, bias, ob, gain, shift):
    n, (tokens, dim) = sizes[1], own.shape
    full = whole((tokens, dim))
    return call(
        functools.partial(attn_fwd_kernel, lens.shape[0], layer), "attn_fwd", side, sizes, cid,
        [lens, win, own, g, bias, ob, gain, shift],
        [SMEM, whole(win.shape), full, per_t((1, dim, dim)), whole(bias.shape)] + [whole(ob.shape)] * 3,
        [sds((n, tokens, 256), BF), sds((n, WIN, 384), BF), sds((n, tokens, 256), BF)]
        + [sds((tokens, dim)), sds((tokens, dim)), sds((tokens, 1))],
        [per_t((1, tokens, 256)), per_t((1, WIN, 384)), per_t((1, tokens, 256)), full, full, whole((tokens, 1))],
        [pltpu.VMEM((tokens, dim), F32)],
    )


def ffn_fwd_kernel(rows, layer, hand_on, me, before, after, mid_ref, up_ref, down_ref, bias_ref, db_ref, gain_ref, shift_ref, *refs):
    act_ref, slope_ref, out_ref, unit_ref, rs_ref, *refs = refs
    if hand_on:
        win_out_ref, acc_ref, low_ref, win_ref, *sems = refs
    else:
        (acc_ref,) = refs
    step, n = pl.program_id(0), pl.num_programs(0)
    dim = mid_ref.shape[1]
    if hand_on:
        @pl.when(step == 0)
        def _():
            win_ref[...] = jnp.zeros(win_ref.shape, BF)
    before(me.beside())
    upper = dot(mid_ref[...].astype(BF), up_ref[0]) + bias_ref[pl.ds(layer * me.n_tensor + step, 1), U_AT : U_AT + dim]
    half = 0.5 + 0.5 * lax.erf(upper * (0.5**0.5))
    act_ref[0] = (upper * half).astype(BF)
    slope_ref[0] = (half + upper * (jnp.exp(-0.5 * upper * upper) * 0.3989422804014327)).astype(BF)
    part = dot_nt(act_ref[0], down_ref[0])

    @pl.when(step == 0)
    def _():
        acc_ref[...] = part

    @pl.when(step > 0)
    def _():
        acc_ref[...] += part

    @pl.when(step == n - 1)
    def _():
        line = pl.ds(layer, 1)
        total = mid_ref[...] + acc_ref[...] + db_ref[line, :]
        out, unit_ref[...], rs_ref[...] = norm_forward(total, gain_ref[line, :], shift_ref[line, :])
        out_ref[...] = out
        if hand_on:
            window = Window(me, mid_ref.shape[0], rows)
            low_ref[...] = out.astype(BF)
            window.send(low_ref, win_ref, sems)
            for j, place in enumerate(window.own_places()):
                win_ref[pl.ds(pl.multiple_of(place * BLK, BLK), BLK), :] = low_ref[pl.ds(j * BLK, BLK), :]
        after()
        if hand_on:
            window.receive(win_ref, sems)
            win_out_ref[...] = win_ref[...]
            window.send(low_ref, win_ref, sems, "wait_send")


def ffn_fwd(side, cid, layer, sizes, rows, mid, g, bias, db, gain, shift):
    n, (tokens, dim) = sizes[1], mid.shape
    hand_on = not isinstance(side, Still)
    full = whole((tokens, dim))
    return call(
        functools.partial(ffn_fwd_kernel, rows, layer, hand_on), "ffn_fwd", side, sizes, cid,
        [mid, g, g, bias, db, gain, shift],
        [full, per_t((1, dim, dim), 0, 0), per_t((1, dim, dim), 0, 1), whole(bias.shape)] + [whole(db.shape)] * 3,
        [sds((n, tokens, dim), BF), sds((n, tokens, dim), BF), sds((tokens, dim)), sds((tokens, dim)), sds((tokens, 1))]
        + ([sds((WIN, dim), BF)] if hand_on else []),
        [per_t((1, tokens, dim)), per_t((1, tokens, dim)), full, full, whole((tokens, 1))]
        + ([whole((WIN, dim))] if hand_on else []),
        [pltpu.VMEM((tokens, dim), F32)]
        + ([pltpu.VMEM((tokens, dim), BF), pltpu.VMEM((WIN, dim), BF)] + Window.sems(tokens) if hand_on else []),
    )


def ffn_bwd_kernel(
    layer, me, before, after, grad_ref, mid_ref, unit2_ref, rs2_ref, unit1_ref, rs1_ref, up_ref, down_ref, act_ref, slope_ref,
    gain1_ref, gain2_ref, dg_ref, ub_ref, dvec_ref, dfirst_ref, acc_ref, low_ref, low_t_ref, mid_t_ref,
):
    step, n = pl.program_id(0), pl.num_programs(0)
    dim = grad_ref.shape[1]
    line = pl.ds(layer, 1)
    before()

    @pl.when(step == 0)
    def _():
        grad = grad_ref[...]
        dsecond = norm_back(grad, unit2_ref[...], rs2_ref[...], gain2_ref[line, :])
        dvec_ref[4:5] = column_sum(grad * unit2_ref[...])
        dvec_ref[5:6] = column_sum(grad)
        dvec_ref[3:4] = column_sum(dsecond)
        dvec_ref[6:8] = jnp.zeros((2, dim), F32)
        acc_ref[...] = dsecond
        low_ref[...] = dsecond.astype(BF)
        low_t_ref[...] = dsecond.T.astype(BF)
        mid_t_ref[...] = mid_ref[...].T.astype(BF)

    dupper = dot(low_ref[...], down_ref[0]) * slope_ref[0].astype(F32)
    ub_ref[0] = column_sum(dupper)
    dupper_low = dupper.astype(BF)
    dg_ref[0, :, 0:dim] = dot(mid_t_ref[...], dupper_low).astype(BF)
    dg_ref[0, :, dim : 2 * dim] = dot(low_t_ref[...], act_ref[0]).astype(BF)
    acc_ref[...] += dot_nt(dupper_low, up_ref[0])

    @pl.when(step == n - 1)
    def _():
        dmid = acc_ref[...]
        dfirst = norm_back(dmid, unit1_ref[...], rs1_ref[...], gain1_ref[line, :])
        dvec_ref[1:2] = column_sum(dmid * unit1_ref[...])
        dvec_ref[2:3] = column_sum(dmid)
        dvec_ref[0:1] = column_sum(dfirst)
        dfirst_ref[...] = dfirst
        after()


def ffn_bwd(side, cid, layer, sizes, grad, mid, unit2, rs2, unit1, rs1, g, act, slope, gain1, gain2):
    n, (tokens, dim) = sizes[1], mid.shape
    full, thin = whole((tokens, dim)), whole((tokens, 1))
    return call(
        functools.partial(ffn_bwd_kernel, layer), "ffn_bwd", side, sizes, cid,
        [grad, mid, unit2, rs2, unit1, rs1, g, g, act, slope, gain1, gain2],
        [full, full, full, thin, full, thin, per_t((1, dim, dim), 0, 0), per_t((1, dim, dim), 0, 1)]
        + [per_t((1, tokens, dim))] * 2 + [whole(gain1.shape)] * 2,
        [sds(g.shape, BF), sds((n, 1, dim)), sds((8, dim)), sds((tokens, dim))],
        [per_t((1, dim, 2 * dim)), per_t((1, 1, dim)), whole((8, dim)), full],
        [
            pltpu.VMEM((tokens, dim), F32), pltpu.VMEM((tokens, dim), BF),
            pltpu.VMEM((dim, tokens), BF), pltpu.VMEM((dim, tokens), BF),
        ],
        early=2,
    )


def attn_bwd_kernel(
    rows, me, before, after, len_ref, dfirst_ref, own_ref, win_ref, g_ref, q_ref, kv_ref, ctx_ref,
    dg_ref, qb_ref, vb_ref, grad_ref, low_ref, low_t_ref, own_t_ref, win_t_ref, dctx_ref, dq_ref, dkv_ref,
    win_grad_ref, win_low_ref, back_ref, *sems,
):
    step, n = pl.program_id(0), pl.num_programs(0)
    tokens = own_ref.shape[0]
    heads = 3
    before(me.beside())

    @pl.when(step == 0)
    def _():
        dfirst = dfirst_ref[...]
        low_ref[...] = dfirst.astype(BF)
        low_t_ref[...] = dfirst.T.astype(BF)
        own_t_ref[...] = flip(own_ref[...])
        win_t_ref[...] = flip(win_ref[...])
        grad_ref[...] = dfirst
        win_grad_ref[...] = jnp.zeros(win_grad_ref.shape, F32)

    dctx_ref[...] = dot(low_ref[...], g_ref[0, :, 128:384]).astype(BF)
    dkv_ref[...] = jnp.zeros(dkv_ref.shape, F32)
    q_masks, c_masks = lane_masks(0, heads), lane_masks(1, heads)
    window = Window(me, tokens, rows)
    for j, (row, slot, part) in enumerate(window.blocks()):
        here = pl.ds(j * BLK, BLK)
        keys = pl.ds(pl.multiple_of(slot * PACK, PACK), PACK)
        q_stack = stack_heads(q_ref[0, here, :], q_masks)
        d_stack = stack_heads(dctx_ref[here, :], c_masks)
        scores = dot_nt(kv_ref[0, keys, 0:256], q_stack) * (HD**-0.5)
        scores = jnp.where(allowed_of(len_ref, row, part * BLK, 0, heads), scores, NEG)
        peak = jnp.max(scores, axis=0, keepdims=True)
        weights = jnp.exp(scores - peak)
        probs = weights * (1.0 / jnp.sum(weights, axis=0, keepdims=True))
        dprobs = dot_nt(kv_ref[0, keys, 128:384], d_stack)
        weighted = probs * dprobs
        inner = jnp.sum(weighted, axis=0, keepdims=True)
        dscores = ((weighted - probs * inner) * (HD**-0.5)).astype(BF)
        dkv_ref[keys, 128:384] += dot(probs.astype(BF), d_stack)
        dkv_ref[keys, 0:256] += dot(dscores, q_stack)
        dq_ref[here, :] = pick_heads(dot_tn(dscores, kv_ref[0, keys, 0:256]), q_masks, BLK)
    dq, dkv = dq_ref[...], dkv_ref[...]
    qb_ref[0] = column_sum(dq)
    vb_ref[0] = column_sum(dkv)
    dq_low, dkv_low = dq.astype(BF), dkv.astype(BF)
    grad_q = dot(own_t_ref[...], dq_low)
    grad_o = dot(low_t_ref[...], ctx_ref[0])
    dg_ref[0, :, 0:128] = grad_q[:, 0:128].astype(BF)
    dg_ref[0, :, 128:256] = (grad_q[:, 128:256] + grad_o[:, 0:128]).astype(BF)
    dg_ref[0, :, 256:384] = grad_o[:, 128:256].astype(BF)
    dg_ref[0, :, 384:768] = dot(win_t_ref[...], dkv_low).astype(BF)
    grad_ref[...] += dot_nt(dq_low, g_ref[0, :, 0:256])
    win_grad_ref[...] += dot_nt(dkv_low, g_ref[0, :, 384:768])

    @pl.when(step == n - 1)
    def _():
        win_low_ref[...] = win_grad_ref[...].astype(BF)
        window.send_back(win_low_ref, back_ref, sems)
        for j, place in enumerate(window.own_places()):
            grad_ref[pl.ds(j * BLK, BLK), :] += win_grad_ref[pl.ds(pl.multiple_of(place * BLK, BLK), BLK), :]
        after()

        def add(j, value):
            grad_ref[pl.ds(j * BLK, BLK), :] += value.astype(F32)

        window.receive_back(back_ref, sems, add)
        window.send_back(win_low_ref, back_ref, sems, "wait_send")


def attn_bwd(side, cid, sizes, lens, dfirst, own, win, g, q, kv, ctx):
    n, (tokens, dim) = sizes[1], own.shape
    full = whole((tokens, dim))
    return call(
        functools.partial(attn_bwd_kernel, lens.shape[0]), "attn_bwd", side, sizes, cid,
        [lens, dfirst, own, win, g, q, kv, ctx],
        [SMEM, full, full, whole(win.shape), per_t((1, dim, dim)), per_t((1, tokens, 256)), per_t((1, WIN, 384)), per_t((1, tokens, 256))],
        [sds(g.shape, BF), sds((n, 1, 256)), sds((n, 1, 384)), sds((tokens, dim))],
        [per_t((1, dim, dim)), per_t((1, 1, 256)), per_t((1, 1, 384)), full],
        [
            pltpu.VMEM((tokens, dim), BF), pltpu.VMEM((dim, tokens), BF), pltpu.VMEM((dim, tokens), BF),
            pltpu.VMEM((dim, WIN), BF), pltpu.VMEM((tokens, 256), BF), pltpu.VMEM((tokens, 256), F32),
            pltpu.VMEM((WIN, 384), F32), pltpu.VMEM((WIN, dim), F32), pltpu.VMEM((WIN, dim), BF),
            pltpu.VMEM((2 * (tokens // BLK), BLK, dim), BF),
        ] + Window.sems(tokens),
        early=2,
    )


def finish_kernel(n_dp, n_tensor, scatter, layers, *refs):
    g_ref, few_refs, refs = refs[0], refs[1 : 1 + 4 * layers], refs[1 + 4 * layers :]
    out_ref, total_ref, part_ref, come_ref, few_send, few_recv, *scratch = refs
    me = Place(n_dp, n_tensor)

    def place_sums():
        part_ref[0] = jnp.zeros(part_ref.shape[1:], F32)
        for l in range(layers):
            dvec, ub, qb, vb = few_refs[4 * l : 4 * l + 4]
            at = 2 * 8 * l
            part_ref[0, at : at + 8, :] = dvec[...]
            for t in range(n_tensor):
                part_ref[0, at + 8 + t : at + 9 + t, :] = ub[t]
                part_ref[0, at + 12 + t : at + 13 + t, 0:256] = qb[t]
                part_ref[0, at + 12 + t : at + 13 + t, 256:640] = vb[t]

    meet(scatter.peers(me))
    turns = scatter.rounds(me, g_ref, out_ref, *scratch)
    few = doubling_sum(me, place_sums, total_ref, part_ref, come_ref, few_send, few_recv)
    for i in range(max(len(turns), len(few))):
        if i < len(turns):
            turns[i]()
        if i < len(few):
            few[i]()


def finish(dg, few, n_dp, n_tensor, layers):
    scatter = Scatter(dg, n_dp, n_tensor)
    rows, cols = scatter.out_shape[0].shape
    shape = (16 * layers, cols)
    return pl.pallas_call(
        functools.partial(finish_kernel, n_dp, n_tensor, scatter, layers),
        in_specs=[HBM] + [VMEM] * len(few),
        out_specs=[VMEM, VMEM],
        out_shape=[sds((rows, cols)), sds(shape)],
        scratch_shapes=doubling_scratch(shape, n_dp, n_tensor) + scatter.scratch,
        compiler_params=pltpu.CompilerParams(vmem_limit_bytes=40 * 1024 * 1024, collective_id=9, has_side_effects=True),
        name="finish",
    )(*scatter.operands, *few)


def body(n_dp, n_tensor, block_input, passage_lengths, qkv_weight, qv_bias, out_weight, out_bias, first_gain,
         first_shift, up_weight, up_bias, down_weight, down_bias, second_gain, second_shift, output_grad):
    layers = qkv_weight.shape[0]
    tokens, dim = block_input.shape
    rows = passage_lengths.shape[0]
    t, dp = lax.axis_index("tensor"), lax.axis_index("dp")
    shard, units = qkv_weight.shape[2], qkv_weight.shape[3]
    hidden_units = up_weight.shape[2]
    sizes = (n_dp, n_tensor)
    lens = passage_lengths

    def flat(g):
        return g.reshape(n_tensor, n_dp * shard, g.shape[-1])

    own = block_input
    a1, f0, f1, win, bias, ga0 = start(qkv_weight, out_weight, up_weight, down_weight, qv_bias, up_bias, own, rows, n_dp, n_tensor)
    ga, gf, kept = [flat(ga0), None], [None, None], []
    for l in range(layers):
        side = Gather(f0 if l == 0 else f1, n_dp, n_tensor)
        q, kv, ctx, mid, unit1, rs1, gathered = attn_fwd(
            side, 1 + 2 * l, l, sizes, lens, win, own, ga[l], bias, out_bias, first_gain, first_shift
        )
        gf[l] = flat(gathered)
        side = Gather(a1, n_dp, n_tensor) if l == 0 else Still()
        act, slope, out, unit2, rs2, *more = ffn_fwd(
            side, 2, l, sizes, rows, mid, gf[l], bias, down_bias, second_gain, second_shift
        )
        kept.append((own, win, q, kv, ctx, mid, unit1, rs1, act, slope, unit2, rs2))
        own = out
        if l == 0:
            win, gathered = more
            ga[1] = flat(gathered)
    block_output = own

    grad = output_grad
    da, few = None, [None] * layers
    sum_f, sum_a = [None] * layers, [None] * layers
    for l in reversed(range(layers)):
        own, win, q, kv, ctx, mid, unit1, rs1, act, slope, unit2, rs2 = kept[l]
        side = Still() if da is None else Scatter(da, n_dp, n_tensor)
        df, ub, dvec, dfirst, *more = ffn_bwd(
            side, 6, l, sizes, grad, mid, unit2, rs2, unit1, rs1, gf[l], act, slope, first_gain, second_gain
        )
        if more:
            sum_a[l + 1] = more[0]
        da, qb, vb, grad, sum_f[l] = attn_bwd(Scatter(df, n_dp, n_tensor), 5 + 2 * l, sizes, lens, dfirst, own, win, ga[l], q, kv, ctx)
        few[l] = [dvec, ub, qb, vb]
    sum_a[0], totals = finish(da, sum(few, []), n_dp, n_tensor, layers)

    totals = totals.reshape(layers, 16, dim)
    piece, wide = qv_bias.shape[2], up_bias.shape[1]
    mine = lax.dynamic_slice(totals, (0, 8 + t, 0), (layers, 1, dim))
    u_grad = lax.dynamic_slice(mine, (0, 0, dp * wide), (layers, 1, wide)).reshape(layers, wide)
    mine = lax.dynamic_slice(totals, (0, 12 + t, 0), (layers, 1, dim))
    q_grad = lax.dynamic_slice(mine, (0, 0, dp * piece), (layers, 1, piece))
    v_grad = lax.dynamic_slice(mine, (0, 0, 256 + units + dp * piece), (layers, 1, piece))
    wa, wf = jnp.stack(sum_a), jnp.stack(sum_f)
    cols = [wa[:, :, i * units : (i + 1) * units] for i in range(4)]
    return (
        block_output,
        grad,
        jnp.stack([cols[0], cols[2], cols[3]], axis=1),
        jnp.concatenate([q_grad, v_grad], axis=1),
        cols[1].transpose(0, 2, 1),
        totals[:, 0],
        totals[:, 1],
        totals[:, 2],
        wf[:, :, :hidden_units],
        u_grad,
        wf[:, :, hidden_units:].transpose(0, 2, 1),
        totals[:, 3],
        totals[:, 4],
        totals[:, 5],
    )


def solution(mesh):
    n_dp, n_tensor = mesh.shape["dp"], mesh.shape["tensor"]
    tokens = P(("dp", "tensor"), None)
    in_specs = (
        tokens, P("dp", None), P(None, None, "dp", "tensor"), P(None, None, ("tensor", "dp")), P(None, "tensor", "dp"),
        P(), P(), P(), P(None, "dp", "tensor"), P(None, ("tensor", "dp")), P(None, "tensor", "dp"), P(), P(), P(), tokens,
    )
    out_specs = (
        tokens, tokens, P(None, None, "dp", "tensor"), P(None, None, ("tensor", "dp")), P(None, "tensor", "dp"),
        P(), P(), P(), P(None, "dp", "tensor"), P(None, ("tensor", "dp")), P(None, "tensor", "dp"), P(), P(), P(),
    )
    return jax.shard_map(
        functools.partial(body, n_dp, n_tensor), mesh=mesh, in_specs=in_specs, out_specs=out_specs, check_vma=False
    )
```

```python
import functools

import jax
import jax.numpy as jnp
from jax import lax
from jax.experimental import pallas as pl
from jax.experimental.pallas import tpu as pltpu
from jax.sharding import PartitionSpec as P

HD = 64
PACK = 512
BLK = 128
PER = PACK // BLK
WIN = 2 * PACK
EPS = 1e-05
NEG = -1e30
MESH = pl.DeviceIdType.MESH
BF = jnp.bfloat16
F32 = jnp.float32
I32 = jnp.int32
HBM = pl.BlockSpec(memory_space=pltpu.MemorySpace.HBM)
VMEM = pl.BlockSpec(memory_space=pltpu.MemorySpace.VMEM)
SMEM = pl.BlockSpec(memory_space=pltpu.MemorySpace.SMEM)
Q_AT, KV_AT = 0, 256


def dot(a, b):
    return jnp.dot(a, b, preferred_element_type=F32)


def dot_nt(a, b):
    return lax.dot_general(a, b, (((1,), (1,)), ((), ())), preferred_element_type=F32)


def dot_tn(a, b):
    return lax.dot_general(a, b, (((0,), (0,)), ((), ())), preferred_element_type=F32)


def whole(shape):
    return pl.BlockSpec(shape, lambda t: (0,) * len(shape))


def per_t(shape, *rest):
    tail = rest if rest else (0,) * (len(shape) - 1)
    return pl.BlockSpec(shape, lambda t: (t,) + tail)


def sds(shape, dtype=F32):
    return jax.ShapeDtypeStruct(shape, dtype)


def column_sum(value):
    return jnp.sum(value, axis=0, keepdims=True)


def flip(value):
    return value.astype(F32).T.astype(BF)


class Place:
    def __init__(self, n_dp, n_tensor):
        self.n_dp, self.n_tensor = n_dp, n_tensor
        self.nz = n_dp // 2
        dp, tensor = lax.axis_index("dp"), lax.axis_index("tensor")
        self.dp, self.tensor = dp, tensor
        self.z, self.y = dp // 2, dp % 2
        self.x, self.c = tensor // 2, tensor % 2
        self.dp_y = 2 * self.z + 1 - self.y
        self.t_x = 2 * (1 - self.x) + self.c
        self.t_c = 2 * self.x + 1 - self.c
        self.t_xc = 2 * (1 - self.x) + 1 - self.c
        self.to_x = (dp, self.t_x)
        self.to_y = (self.dp_y, tensor)
        self.to_c = (dp, self.t_c)

    def d(self, z, same_y=True):
        return 2 * z + (self.y if same_y else 1 - self.y)

    def near(self):
        return [(self.to_x, None), (self.to_y, None), (self.to_c, None)]

    def along_z(self):
        return [((self.dp - 2, self.tensor), self.z > 0), ((self.dp + 2, self.tensor), self.z < self.nz - 1)]

    def far_z(self):
        return [((self.dp ^ (2 << b), self.tensor), None) for b in range(1, bits(self.nz))]

    def beside(self):
        other = self.tensor - 1 + 2 * self.c
        return [((self.dp, other), jnp.logical_and(other >= 0, other < self.n_tensor))]


def meet(peers):
    barrier = pltpu.get_barrier_semaphore()
    count = 0
    for device, valid in peers:
        def signal(device=device):
            pl.semaphore_signal(barrier, inc=1, device_id=device, device_id_type=MESH)
        if valid is None:
            signal()
            count = count + 1
        else:
            pl.when(valid)(signal)
            count = count + valid.astype(I32)
    return lambda: pl.semaphore_wait(barrier, count)


def bits(n):
    return n.bit_length() - 1


def pairs(me):
    found = [(me.dp, me.tensor ^ (1 << b)) for b in range(bits(me.n_tensor))]
    return found + [(me.dp ^ (1 << b), me.tensor) for b in range(bits(me.n_dp))]


def rounds_of(n_dp, n_tensor):
    return bits(n_dp) + bits(n_tensor)


def doubling_sum(me, first, total_ref, part_ref, come_ref, send_sem, recv_sem):
    copies = [
        pltpu.make_async_remote_copy(
            src_ref=part_ref.at[i], dst_ref=come_ref.at[i], send_sem=send_sem.at[i], recv_sem=recv_sem.at[i],
            device_id=device, device_id_type=MESH,
        )
        for i, device in enumerate(pairs(me))
    ]

    def begin():
        first()
        copies[0].start()

    def middle(i):
        copies[i].wait_recv()
        total = part_ref[i] + come_ref[i]
        if i + 1 < len(copies):
            part_ref[i + 1] = total
            copies[i + 1].start()
        else:
            total_ref[...] = total

    def end():
        for copy in copies:
            copy.wait_send()

    return [begin] + [functools.partial(middle, i) for i in range(len(copies))] + [end]


def doubling_scratch(shape, n_dp, n_tensor):
    n = rounds_of(n_dp, n_tensor)
    return [
        pltpu.VMEM((n,) + shape, F32), pltpu.VMEM((n,) + shape, F32),
        pltpu.SemaphoreType.DMA((n,)), pltpu.SemaphoreType.DMA((n,)),
    ]


class Window:
    def __init__(self, me, tokens, rows):
        self.me, self.count, self.rows = me, tokens // BLK, rows

    def first(self, t):
        return jnp.minimum(t * self.count // PER, self.rows - 2)

    def blocks(self):
        t = self.me.tensor
        found = []
        for j in range(self.count):
            g = t * self.count + j
            found.append((g // PER, g // PER - self.first(t), g % PER))
        return found

    def needed(self, source, j, target):
        g = source * self.count + j
        row = g // PER
        inside = jnp.logical_and(row >= target * self.count // PER, row <= (target * self.count + self.count - 1) // PER)
        exists = jnp.logical_and(jnp.logical_and(source >= 0, source < self.me.n_tensor),
                                 jnp.logical_and(target >= 0, target < self.me.n_tensor))
        return jnp.logical_and(inside, exists), g - self.first(target) * PER

    def own_places(self):
        t = self.me.tensor
        return [t * self.count + j - self.first(t) * PER for j in range(self.count)]

    def _each(self, outgoing):
        t = self.me.tensor
        for i, step in enumerate((1, -1)):
            for j in range(self.count):
                source, target = (t, t + step) if outgoing else (t - step, t)
                valid, place = self.needed(source, j, target)
                yield i * self.count + j, j, source, target, valid, pl.multiple_of(place * BLK, BLK)

    def _copy(self, source, target, slot, device, sems):
        return pltpu.make_async_remote_copy(
            src_ref=source, dst_ref=target, send_sem=sems[0].at[slot], recv_sem=sems[1].at[slot],
            device_id=(self.me.dp, device), device_id_type=MESH,
        )

    def send(self, low_ref, win_ref, sems, what="start"):
        for slot, j, source, target, valid, place in self._each(True):
            copy = self._copy(low_ref.at[pl.ds(j * BLK, BLK)], win_ref.at[pl.ds(place, BLK)], slot, target, sems)
            pl.when(valid)(getattr(copy, what))

    def receive(self, win_ref, sems):
        for slot, j, source, target, valid, place in self._each(False):
            here = win_ref.at[pl.ds(place, BLK)]
            pl.when(valid)(pltpu.make_async_copy(here, here, sems[1].at[slot]).wait)

    def send_back(self, grad_ref, back_ref, sems, what="start"):
        for slot, j, source, target, valid, place in self._each(False):
            copy = self._copy(grad_ref.at[pl.ds(place, BLK)], back_ref.at[slot], slot, source, sems)
            pl.when(valid)(getattr(copy, what))

    def receive_back(self, back_ref, sems, add):
        for slot, j, source, target, valid, place in self._each(True):
            def take(slot=slot, j=j):
                pltpu.make_async_copy(back_ref.at[slot], back_ref.at[slot], sems[1].at[slot]).wait()
                add(j, back_ref[slot])
            pl.when(valid)(take)

    def sems(tokens):
        n = 2 * (tokens // BLK)
        return [pltpu.SemaphoreType.DMA((n,)), pltpu.SemaphoreType.DMA((n,))]


class Gather:
    def __init__(self, n_dp):
        self.slots = 12 * (n_dp // 2)

    def scratch(self):
        return [pltpu.SemaphoreType.DMA, pltpu.SemaphoreType.DMA((self.slots,)), pltpu.SemaphoreType.DMA((self.slots,))]

    def rounds(self, me, own_ref, out_ref, own_sem, send_sem, recv_sem):
        nz, cols = me.nz, own_ref.shape[-1]
        sixth = cols // 6 // 128 * 128
        cuts = {0: (0, cols // 2), 1: (cols // 2, cols), 2: (0, sixth), 3: (sixth, 2 * sixth), 4: (2 * sixth, cols)}

        def piece(r, d, part):
            if part is None:
                return out_ref.at[r, d]
            lo, hi = cuts[part]
            return out_ref.at[r, d, :, pl.ds(lo, hi - lo)]

        def copy(source, r, d, part, turn, route, p, device):
            slot = route * nz + p
            return pltpu.make_async_remote_copy(
                src_ref=source if source is not None else piece(r, d, part), dst_ref=piece(r ^ turn, d, part),
                send_sem=send_sem.at[slot], recv_sem=recv_sem.at[slot], device_id=device, device_id_type=MESH,
            )

        def arrived(r, d, part, route, p):
            pltpu.make_async_copy(piece(r, d, part), piece(r, d, part), recv_sem.at[route * nz + p]).wait()

        mine = pltpu.make_async_copy(own_ref, out_ref.at[0, me.dp], own_sem)
        up, down = (me.dp + 2, me.tensor), (me.dp - 2, me.tensor)
        can_up, can_down = me.z < nz - 1, me.z > 0

        def z_copy(p, upward, source=None):
            return copy(source, 0, me.d(p), None, 0, 0 if upward else 1, p, up if upward else down)

        def x_copy(p, source=None):
            return copy(source, 0, me.d(p), None, 2, 2, p, me.to_x)

        def y_copy(p, source=None):
            return copy(source, 0, me.d(p), None, 0, 3, p, me.to_y)

        def first_copy(p, here):
            return copy(None, 2, me.d(p), 0 if here else 2, 0, 4, p, me.to_y)

        def second_copy(p, here):
            return copy(None, 0, me.d(p, False), 1 if here else 3, 2, 5, p, me.to_x)

        def diagonal_z(p, upward):
            return copy(None, 2, me.d(p, False), 4, 0, 6 if upward else 7, p, up if upward else down)

        def core_copy(kind, p, source=None):
            return copy(source, 0 if kind in (0, 2) else 2, me.d(p, kind in (0, 1)), None, 1, 8 + kind, p, me.to_c)

        def own_round():
            mine.start()
            pl.when(can_up)(z_copy(me.z, True, own_ref).start)
            pl.when(can_down)(z_copy(me.z, False, own_ref).start)
            x_copy(me.z, own_ref).start()
            y_copy(me.z, own_ref).start()
            core_copy(0, me.z, own_ref).start()

        def z_round(p, upward, valid):
            @pl.when(valid)
            def _():
                arrived(0, me.d(p), None, 0 if upward else 1, p)
                pl.when(can_up if upward else can_down)(z_copy(p, upward).start)
                x_copy(p).start()
                y_copy(p).start()
                core_copy(0, p).start()

        def xy_round(p, here, valid=None):
            def go():
                arrived(2, me.d(p), None, 2, p)
                first_copy(p, here).start()
                core_copy(1, p).start()
                arrived(0, me.d(p, False), None, 3, p)
                second_copy(p, here).start()
                core_copy(2, p).start()
            go() if valid is None else pl.when(valid)(go)

        def diagonal_here():
            arrived(2, me.d(me.z, False), 0, 4, me.z)
            arrived(2, me.d(me.z, False), 1, 5, me.z)
            pl.when(can_up)(diagonal_z(me.z, True).start)
            pl.when(can_down)(diagonal_z(me.z, False).start)
            core_copy(3, me.z).start()

        def diagonal_round(p, upward, valid):
            @pl.when(valid)
            def _():
                arrived(2, me.d(p, False), 4, 6 if upward else 7, p)
                pl.when(can_up if upward else can_down)(diagonal_z(p, upward).start)
                arrived(2, me.d(p, False), 2, 4, p)
                arrived(2, me.d(p, False), 3, 5, p)
                core_copy(3, p).start()

        def middle(s):
            low, high = me.z - s, me.z + s
            if s < nz:
                z_round(low, True, low >= 0)
                z_round(high, False, high < nz)
            if s == 1:
                xy_round(me.z, True)
            elif s - 1 < nz:
                xy_round(low + 1, False, low + 1 >= 0)
                xy_round(high - 1, False, high - 1 < nz)
            if s == 2:
                diagonal_here()
            elif 2 < s < nz + 2:
                diagonal_round(low + 2, True, low + 2 >= 0)
                diagonal_round(high - 2, False, high - 2 < nz)

        def several(start, stop):
            for s in range(start, stop):
                middle(s)

        def from_core(kinds):
            for p in range(nz):
                for kind in kinds:
                    arrived(1 if kind in (0, 2) else 3, me.d(p, kind in (0, 1)), None, 8 + kind, p)

        def end():
            for p in range(nz):
                here = me.z == p
                pl.when(jnp.logical_and(can_up, p <= me.z))(z_copy(p, True).wait_send)
                pl.when(jnp.logical_and(can_down, p >= me.z))(z_copy(p, False).wait_send)
                x_copy(p).wait_send()
                y_copy(p).wait_send()
                for made in (first_copy, second_copy):
                    pl.when(here)(made(p, True).wait_send)
                    pl.when(jnp.logical_not(here))(made(p, False).wait_send)
                pl.when(jnp.logical_and(can_up, p <= me.z))(diagonal_z(p, True).wait_send)
                pl.when(jnp.logical_and(can_down, p >= me.z))(diagonal_z(p, False).wait_send)
                for kind in range(4):
                    core_copy(kind, p).wait_send()

        third = (nz - 1) // 3
        return {
            "T0": own_round,
            "T1": functools.partial(several, 1, 1 + third),
            "T2": functools.partial(several, 1 + third, 1 + 2 * third),
            "T3": functools.partial(several, 1 + 2 * third, nz),
            "T4": lambda: (mine.wait(), middle(nz)),
            "T5": functools.partial(middle, nz + 1),
            "E1": functools.partial(from_core, (0, 2)),
            "E3": functools.partial(from_core, (1, 3)),
            "E": end,
        }


class Scatter:
    def __init__(self, n_dp, rows, cols, sets):
        self.nz, self.rows, self.cols, self.sets = n_dp // 2, rows, cols, sets

    def buffers(self):
        nz, rows, cols, sets = self.nz, self.rows, self.cols, self.sets
        return [
            pltpu.VMEM((2 * sets, 2 * nz, rows, cols), BF),
            pltpu.VMEM((2 * nz, rows, cols), BF),
            pltpu.VMEM((sets, nz, rows, cols // 2), BF),
            pltpu.VMEM((sets, nz, rows, cols // 2), BF),
            pltpu.VMEM((sets, nz, rows, cols), BF),
            pltpu.VMEM((sets, nz, rows, cols), BF),
            pltpu.VMEM((sets, nz - 1, rows, cols), BF),
            pltpu.VMEM((sets, rows, cols), F32),
        ]

    def block(self, layer, block):
        return 2 * layer + block if self.sets > 1 else block

    def sems(self, layers):
        return [
            pltpu.SemaphoreType.DMA((layers, 5 * self.nz + 2)), pltpu.SemaphoreType.DMA((layers, 5 * self.nz + 2)),
            pltpu.SemaphoreType.DMA((layers,)), pltpu.SemaphoreType.REGULAR,
        ]

    def order(self, me):
        return [lax.rem(me.z + k, me.nz) for k in range(1, me.nz)] + [me.z]

    def peers(self, me):
        return me.near() + [((me.d(z), me.tensor), None) for z in self.order(me)[:-1]]

    def core(self, me, buffers, sems, layer, block):
        sums, stage = buffers[:2]
        slot = 5 * self.nz + block
        return pltpu.make_async_remote_copy(
            src_ref=stage, dst_ref=sums.at[self.block(layer, block)], send_sem=sems[0].at[layer, slot], recv_sem=sems[1].at[layer, slot],
            device_id=me.to_c, device_id_type=MESH,
        )

    def wait_credit(self, me, sems):
        pl.semaphore_wait(sems[3], len(self.peers(me)))

    def rounds(self, me, buffers, sems, layer, out_ref):
        which = layer if self.sets > 1 else 0
        sums, _, *rest = buffers
        sums = sums.at[pl.ds(2 * which, 2)]
        first_in, second_in, x_in, y_in, z_in, total_ref = [item.at[which] for item in rest]
        send_sem, recv_sem, out_sem, credit = sems
        nz = self.nz
        half = self.cols // 2
        zs = self.order(me)

        def remote(source, target, slot, device):
            return pltpu.make_async_remote_copy(
                src_ref=source, dst_ref=target, send_sem=send_sem.at[layer, slot], recv_sem=recv_sem.at[layer, slot],
                device_id=device, device_id_type=MESH,
            )

        def first(k):
            return remote(sums.at[1, me.d(zs[k], False), :, pl.ds(0, half)], first_in.at[k], k, me.to_x)

        def second(k):
            return remote(sums.at[1, me.d(zs[k], False), :, pl.ds(half, half)], second_in.at[k], nz + k, me.to_y)

        def along_x(k):
            return remote(sums.at[1, me.d(zs[k])], x_in.at[k], 2 * nz + k, me.to_x)

        def along_y(k):
            return remote(sums.at[0, me.d(zs[k], False)], y_in.at[k], 3 * nz + k, me.to_y)

        def along_z(k):
            return remote(sums.at[0, me.d(zs[k])], z_in.at[k], 4 * nz + k, (me.d(zs[k]), me.tensor))

        def diagonals():
            for k in range(nz):
                first(k).start()
                second(k).start()

        def x_turn(k):
            second(k).wait_recv()
            d = me.d(zs[k])
            sums[1, d, :, half:] = (sums[1, d, :, half:].astype(F32) + second_in[k].astype(F32)).astype(BF)
            along_x(k).start()

        def y_turn(k):
            first(k).wait_recv()
            d = me.d(zs[k], False)
            sums[0, d, :, :half] = (sums[0, d, :, :half].astype(F32) + first_in[k].astype(F32)).astype(BF)
            along_y(k).start()

        def z_sum(k):
            along_x(k).wait_recv()
            along_y(k).wait_recv()
            return sums[0, me.d(zs[k])].astype(F32) + x_in[k].astype(F32) + y_in[k].astype(F32)

        def z_turn(k):
            sums[0, me.d(zs[k])] = z_sum(k).astype(BF)
            along_z(k).start()

        def last():
            total = z_sum(nz - 1)
            for k in range(nz - 1):
                along_z(k).wait_recv()
                total += z_in[k].astype(F32)
            total_ref[...] = total
            pltpu.make_async_copy(total_ref, out_ref, out_sem.at[layer]).start()

        def end():
            for k in range(nz):
                for made in (first, second, along_x, along_y):
                    made(k).wait_send()
                if k < nz - 1:
                    along_z(k).wait_send()
            pltpu.make_async_copy(total_ref, out_ref, out_sem.at[layer]).wait()

        def give_credit():
            for device, _ in self.peers(me):
                pl.semaphore_signal(credit, inc=1, device_id=device, device_id_type=MESH)

        def several(turn, start, stop):
            for k in range(start, stop):
                turn(k)

        found = {"D": diagonals, "L": last, "E": end}
        if self.sets == 1:
            found["C"] = give_credit
        for name, turn, count, parts in (("X", x_turn, nz, 4), ("Y", y_turn, nz, 4), ("Z", z_turn, nz - 1, 3)):
            for i in range(parts):
                found[name + str(i)] = functools.partial(several, turn, count * i // parts, count * (i + 1) // parts)
        return found


def ends_of(len_ref, row):
    total, ends = 0, []
    for k in range(len_ref.shape[1]):
        total = total + len_ref[row, k]
        ends.append(total)
    return ends


def segments(ends, place):
    seg = jnp.zeros(place.shape, I32)
    for end in ends:
        seg += (place >= end).astype(I32)
    return jnp.where(seg == len(ends), -1, seg)


def allowed_of(len_ref, row, offset, key_axis, heads):
    ends = ends_of(len_ref, row)
    k_shape = (1, PACK) if key_axis == 1 else (PACK, 1)
    q_shape = (BLK, 1) if key_axis == 1 else (1, BLK)
    kseg = segments(ends, lax.broadcasted_iota(I32, k_shape, key_axis))
    qseg = segments(ends, lax.broadcasted_iota(I32, q_shape, 1 - key_axis) + offset)
    allowed = jnp.logical_and(kseg >= 0, jnp.logical_or(kseg == qseg, qseg < 0))
    return jnp.concatenate([allowed] * heads, axis=1 - key_axis)


def lane_masks(first, count):
    slot = lax.broadcasted_iota(jnp.int32, (1, 256), 1) // HD
    return [(slot == first + i).astype(F32).astype(BF) for i in range(count)]


def stack_heads(block, masks):
    return jnp.concatenate([block * mask for mask in masks], axis=0)


def pick_heads(stacked, masks, size):
    total = None
    for i, mask in enumerate(masks):
        part = stacked[i * size : (i + 1) * size] * mask.astype(F32)
        total = part if total is None else total + part
    return total


def norm_forward(value, gain, shift):
    average = jnp.mean(value, axis=-1, keepdims=True)
    centered = value - average
    variance = jnp.mean(centered * centered, axis=-1, keepdims=True)
    scaled = lax.rsqrt(variance + EPS)
    unit = centered * scaled
    return unit * gain + shift, unit, scaled


def norm_back(grad, unit, scaled, gain):
    inner = grad * gain
    centered = inner - jnp.mean(inner, axis=-1, keepdims=True)
    return scaled * (centered - unit * jnp.mean(inner * unit, axis=-1, keepdims=True))


PLAN = [
    [
        "A0T0", "B0T0", "F0T0", "A0T1", "B0T1", "A0T2", "B0T2", "A1T0", "A0T3", "B0T3", "F0T1",
        "W0", "A0T4", "B0T4", "A0E1", "B0E1", "F0T2", "A1T1", "R0", "A0T5", "B0T5",
    ],
    ["F0T3"],
    ["A0E3", "B0E3", "F1T0"],
    ["F0T4", "A1T2"],
    ["F0E1", "F1T1"],
    ["F0T5"],
    [],
    ["A1T3", "F0E3"],
    ["A1T4", "F1T2", "A1E1", "R1"],
    ["A1T5"],
    ["A1E3", "F1T3"],
    [],
    ["F1T4"],
    ["F1E1"],
    ["F1T5"],
    ["F1E3"],
]


def forward_kernel(
    n_dp, n_tensor, len_ref, qkv_ref, ow_ref, up_ref, down_ref, qvb_ref, ub_ref, own_ref,
    ob_ref, gain1_ref, shift1_ref, db_ref, gain2_ref, shift2_ref,
    q_ref, kv_ref, ctx_ref, act_ref, slope_ref, mid_ref, unit1_ref, rs1_ref, unit2_ref, rs2_ref, out_ref,
    win_out_ref, ga_ref, gf_ref,
    gb_ref, a_ref, f_ref, b_ref, wa_ref, wf_ref, wb_ref, h_ref, acc_ref, low_ref, win_ref, bias_ref,
    wa_sem, wf_sem, wb_sem, win_sem, win_send, win_recv, *gather_sems,
):
    me = Place(n_dp, n_tensor)
    step, n = pl.program_id(0), n_tensor
    layers = qkv_ref.shape[0]
    tokens, dim = own_ref.shape
    rows = len_ref.shape[0]
    heads = 3
    layer, phase, r = step // (2 * n), step // n % 2, step % n
    vec = pl.ds(layer, 1)
    window = Window(me, tokens, rows)
    own_rows = pl.ds(pl.multiple_of(window.own_places()[0] * BLK, BLK), tokens)
    gather = Gather(n_dp)
    waves = {}
    for i, name in enumerate(("A0", "F0", "A1", "F1")):
        own, out = ((a_ref, ga_ref), (f_ref, gf_ref))[i % 2]
        for key, turn in gather.rounds(me, own.at[i // 2], out.at[i // 2], *gather_sems[3 * i : 3 * i + 3]).items():
            waves[name + key] = turn
    for key, turn in gather.rounds(me, b_ref, gb_ref, *gather_sems[12:15]).items():
        waves["B0" + key] = turn

    def window_sems(l):
        return win_send.at[l], win_recv.at[l]

    def pack_a(l):
        units = qkv_ref.shape[3]
        a_ref[l, :, 0:units] = qkv_ref[l, 0]
        a_ref[l, :, units : 2 * units] = flip(ow_ref[l])
        a_ref[l, :, 2 * units : 3 * units] = qkv_ref[l, 1]
        a_ref[l, :, 3 * units : 4 * units] = qkv_ref[l, 2]

    def pack_f(l):
        units = up_ref.shape[2]
        f_ref[l, :, 0:units] = up_ref[l]
        f_ref[l, :, units : 2 * units] = down_ref[l]

    def pack_b():
        piece, wide = qvb_ref.shape[2], ub_ref.shape[1]
        units = qkv_ref.shape[3]

        def spread(values, start):
            size = values.shape[1]
            source = lax.broadcasted_iota(I32, (size, dim), 0)
            target = lax.broadcasted_iota(I32, (size, dim), 1)
            return dot(values, (target == source + start).astype(F32).astype(BF))

        u = spread(ub_ref[...], me.dp * wide)
        place = lax.broadcasted_iota(I32, b_ref.shape, 0)
        total = jnp.zeros(b_ref.shape, F32)
        for l in range(layers):
            row = spread(qvb_ref[l], Q_AT + me.dp * piece)[0:1]
            row += spread(qvb_ref[l], KV_AT + units + me.dp * piece)[1:2]
            total += jnp.where(place == 2 * l, row, 0.0) + jnp.where(place == 2 * l + 1, u[l : l + 1], 0.0)
        b_ref[...] = total.astype(BF)

    def hand_on(l):
        window.send(low_ref, win_ref.at[l], window_sems(l))
        for j, place in enumerate(window.own_places()):
            win_ref[l, pl.ds(pl.multiple_of(place * BLK, BLK), BLK), :] = low_ref[pl.ds(j * BLK, BLK), :]

    def take_on(l):
        window.receive(win_ref.at[l], window_sems(l))
        window.send(low_ref, win_ref.at[l], window_sems(l), "wait_send")
        pltpu.make_async_copy(win_ref.at[l], win_out_ref.at[l], win_sem.at[l]).start()

    waves["R1"] = lambda: take_on(1)
    waves["W0"] = lambda: hand_on(0)
    waves["R0"] = lambda: take_on(0)

    def load(s):
        l, p, i = s // (2 * n), s // n % 2, s % n
        if p == 1:
            return [pltpu.make_async_copy(gf_ref.at[l, i], wf_ref.at[i % 2], wf_sem.at[i % 2])]
        copies = [pltpu.make_async_copy(ga_ref.at[l, i], wa_ref.at[i % 2], wa_sem.at[i % 2])]
        if l == 0:
            copies.append(pltpu.make_async_copy(gb_ref.at[i], wb_ref.at[i % 2], wb_sem.at[i % 2]))
        return copies

    def here(s):
        l, p, i = s // (2 * n), s // n % 2, s % n
        name = "AF"[p] + str(l) + ("T4", "E1", "T5", "E3")[i]
        return [k for k, names in enumerate(PLAN) if name in names][0]

    for s, names in enumerate(PLAN):
        @pl.when(step == s)
        def _(s=s, names=names):
            if s == 0:
                win_ref[...] = jnp.zeros(win_ref.shape, BF)
                met = meet(me.near() + me.along_z() + me.beside())
                for l in range(layers):
                    pack_a(l)
                    pack_f(l)
                pack_b()
                low_ref[...] = own_ref[...]
                h_ref[...] = own_ref[...].astype(F32)
                met()
            for name in names:
                waves[name]()
            begun = [k for k in (s, s + 1) if k < len(PLAN) and max(here(k), k - 1) == s]
            for k in begun:
                for copy in load(k):
                    copy.start()
            for copy in load(s):
                copy.wait()

    @pl.when(phase == 0)
    def _():
        slot = r % 2

        @pl.when(layer == 0)
        def _():
            bias_ref[r] = jnp.sum(wb_ref[slot].astype(F32), axis=0)

        def weights(lo, hi):
            return wa_ref[slot, :, :, lo:hi].reshape(dim, hi - lo)

        kv_ref[0, 0] = (dot(win_ref[layer], weights(384, 768)) + bias_ref[r, pl.ds(2 * layer, 1), KV_AT : KV_AT + 384]).astype(BF)
        q_ref[0, 0] = (dot(win_ref[layer, own_rows, :], weights(0, 256)) + bias_ref[r, pl.ds(2 * layer, 1), Q_AT : Q_AT + 256]).astype(BF)
        q_masks, c_masks = lane_masks(0, heads), lane_masks(1, heads)
        for j, (row, place, part) in enumerate(window.blocks()):
            here = pl.ds(j * BLK, BLK)
            keys = pl.ds(pl.multiple_of(place * PACK, PACK), PACK)
            stacked = stack_heads(q_ref[0, 0, here, :], q_masks)
            scores = dot_nt(stacked, kv_ref[0, 0, keys, 0:256]) * (HD**-0.5)
            scores = jnp.where(allowed_of(len_ref, row, part * BLK, 1, heads), scores, NEG)
            peak = jnp.max(scores, axis=-1, keepdims=True)
            exps = jnp.exp(scores - peak)
            probs = exps * (1.0 / jnp.sum(exps, axis=-1, keepdims=True))
            out = dot(probs.astype(BF), kv_ref[0, 0, keys, 128:384])
            ctx_ref[0, 0, here, :] = pick_heads(out, c_masks, BLK).astype(BF)
        part = dot_nt(ctx_ref[0, 0], weights(128, 384))

        @pl.when(r == 0)
        def _():
            acc_ref[...] = part

        @pl.when(r > 0)
        def _():
            acc_ref[...] += part

        @pl.when(r == n - 1)
        def _():
            total = h_ref[...] + acc_ref[...] + ob_ref[vec, :]
            h_ref[...], unit, rs1_ref[0] = norm_forward(total, gain1_ref[vec, :], shift1_ref[vec, :])
            unit1_ref[0] = unit.astype(BF)
            low_ref[...] = h_ref[...].astype(BF)
            mid_ref[0] = low_ref[...]

    @pl.when(phase == 1)
    def _():
        slot = r % 2

        def weights(lo, hi):
            return wf_ref[slot, :, :, lo:hi].reshape(dim, hi - lo)

        upper = dot(low_ref[...], weights(0, dim)) + bias_ref[r, pl.ds(2 * layer + 1, 1), :]
        half = 0.5 + 0.5 * lax.erf(upper * (0.5**0.5))
        act_ref[0, 0] = (upper * half).astype(BF)
        slope_ref[0, 0] = (half + upper * (jnp.exp(-0.5 * upper * upper) * 0.3989422804014327)).astype(BF)
        part = dot_nt(act_ref[0, 0], weights(dim, 2 * dim))

        @pl.when(r == 0)
        def _():
            acc_ref[...] = part

        @pl.when(r > 0)
        def _():
            acc_ref[...] += part

        @pl.when(r == n - 1)
        def _():
            total = h_ref[...] + acc_ref[...] + db_ref[vec, :]
            out, unit, rs2_ref[0] = norm_forward(total, gain2_ref[vec, :], shift2_ref[vec, :])
            unit2_ref[0] = unit.astype(BF)
            h_ref[...] = out

    @pl.when(step == 2 * n - 1)
    def _():
        low_ref[...] = h_ref[...].astype(BF)
        hand_on(1)

    @pl.when(step == pl.num_programs(0) - 1)
    def _():
        out_ref[...] = h_ref[...]
        for name in ("A0", "B0", "F0", "A1", "F1"):
            waves[name + "E"]()
        for l in range(layers):
            pltpu.make_async_copy(win_ref.at[l], win_out_ref.at[l], win_sem.at[l]).wait()


def forward(lens, qkv, ow, up, down, qvb, ub, own, vecs, n_dp, n_tensor):
    layers, _, shard, units = qkv.shape
    (tokens, dim), n = own.shape, n_tensor
    hidden = up.shape[2]
    a_cols, f_cols = 4 * units, 2 * hidden
    biases = (16, dim)
    gather = Gather(n_dp)
    blocks = 2 * (tokens // BLK)

    def in_attn(shape):
        def at(s):
            i = s // (2 * n) * n + jnp.where(s // n % 2 == 0, s % n, n - 1)
            return (i // n, i % n, 0, 0)
        return pl.BlockSpec((1, 1) + shape, at)

    def in_ffn(shape):
        def at(s):
            i = jnp.maximum(s // (2 * n) * n + jnp.where(s // n % 2 == 1, s % n, -1), 0)
            return (i // n, i % n, 0, 0)
        return pl.BlockSpec((1, 1) + shape, at)

    def per_layer(shape):
        return pl.BlockSpec((1,) + shape, lambda s: (s // (2 * n), 0, 0))

    operands = [lens, qkv, ow, up, down, qvb, ub, own] + vecs
    return pl.pallas_call(
        functools.partial(forward_kernel, n_dp, n_tensor),
        grid=(2 * n * layers,),
        in_specs=[SMEM] + [whole(item.shape) for item in operands[1:]],
        out_specs=[
            in_attn((tokens, 256)), in_attn((WIN, 384)), in_attn((tokens, 256)), in_ffn((tokens, hidden)), in_ffn((tokens, hidden)),
            per_layer((tokens, dim)), per_layer((tokens, dim)), per_layer((tokens, 1)), per_layer((tokens, dim)), per_layer((tokens, 1)),
            whole((tokens, dim)), HBM, HBM, HBM, HBM,
        ],
        out_shape=[
            sds((layers, n, tokens, 256), BF), sds((layers, n, WIN, 384), BF), sds((layers, n, tokens, 256), BF),
            sds((layers, n, tokens, hidden), BF), sds((layers, n, tokens, hidden), BF),
            sds((layers, tokens, dim), BF), sds((layers, tokens, dim), BF), sds((layers, tokens, 1)),
            sds((layers, tokens, dim), BF), sds((layers, tokens, 1)), sds((tokens, dim)), sds((layers, WIN, dim), BF),
            sds((layers, n, n_dp, shard, a_cols), BF), sds((layers, n, n_dp, shard, f_cols), BF),
            sds((n, n_dp) + biases, BF),
        ],
        scratch_shapes=[
            pltpu.VMEM((layers, shard, a_cols), BF), pltpu.VMEM((layers, shard, f_cols), BF), pltpu.VMEM(biases, BF),
            pltpu.VMEM((2, n_dp, shard, a_cols), BF), pltpu.VMEM((2, n_dp, shard, f_cols), BF), pltpu.VMEM((2, n_dp) + biases, BF),
            pltpu.VMEM((tokens, dim), F32), pltpu.VMEM((tokens, dim), F32), pltpu.VMEM((tokens, dim), BF),
            pltpu.VMEM((layers, WIN, dim), BF), pltpu.VMEM((n,) + biases, F32),
        ]
        + [pltpu.SemaphoreType.DMA((2,))] * 3 + [pltpu.SemaphoreType.DMA((layers,))]
        + [pltpu.SemaphoreType.DMA((layers, blocks))] * 2
        + gather.scratch() * 5,
        compiler_params=pltpu.CompilerParams(vmem_limit_bytes=60 * 1024 * 1024, collective_id=0, has_side_effects=True),
        name="forward",
    )(*operands)


PLAN_BACK = [
    [],
    [],
    ["F1D"],
    [],
    ["F1X0", "F1Y0"],
    ["F1Y1", "F1X1", "F1X2"],
    ["A1D"],
    ["F1Z0"],
    ["A1Y0", "A1Y1", "A1Y2", "A1X0", "A1X1", "F1Z1", "A1Y3", "A1X2", "R1", "F1Y2"],
    ["A1Z0", "A1X3", "A1Z1"],
    ["F0D", "A1Z2"],
    [],
    [
        "A1L", "F0Y0", "F0Y1", "S0", "F0X0", "F1Z2", "F0X1", "A1E", "A1C", "F0Y2", "S1",
        "F0X2",
    ],
    ["F0Z0"],
    ["F0Z1", "A0D"],
    ["S2", "A0X0"],
]
LAST_BACK = [
    "S3", "A0Y0", "Q0", "A0Y1", "A0X1", "F0Z2", "R0", "Q1", "A0Y2", "A0Y3", "A0Z0",
    "A0X2", "Q2", "F0X3", "A0Z1", "A0X3", "F0Y3", "Q3", "A0Z2", "F1X3", "F1Y3", "S4",
    "F0L", "Q4", "A0L", "F1L", "Q5", "S5",
]


def backward_kernel(
    n_dp, n_tensor, len_ref, grad_in_ref, up_ref, down_ref, g_ref, act_ref, slope_ref, q_ref, kv_ref, ctx_ref,
    mid_ref, unit1_ref, rs1_ref, unit2_ref, rs2_ref, win_ref, gain1_ref, gain2_ref,
    grad_out_ref, sum_f_ref, sum_a_ref, few_ref,
    grad_ref, acc_ref, low_ref, low_t_ref, own_t_ref, win_t_ref, dctx_ref, dq_ref, dkv_ref, win_grad_ref, win_low_ref, back_ref,
    part_ref, come_ref, few_send, few_recv, late_part_ref, late_come_ref, late_send, late_recv, early_ref, late_ref, rows_ref,
    back_send, back_recv, grad_sem, win_sem, *scratch,
):
    me = Place(n_dp, n_tensor)
    step, n = pl.program_id(0), n_tensor
    layers = few_ref.shape[0] // 16
    tokens, dim = grad_ref.shape
    rows = len_ref.shape[0]
    heads = 3
    layer, phase, r = layers - 1 - step // (2 * n), step // n % 2, n - 1 - step % n
    line, at = pl.ds(layer, 1), layer * 16
    mine = me.tensor ^ r
    window = Window(me, tokens, rows)
    own_rows = pl.ds(pl.multiple_of(window.own_places()[0] * BLK, BLK), tokens)
    shard = dim // n_dp
    kinds = {"F": Scatter(n_dp, shard, 2 * dim, layers), "A": Scatter(n_dp, shard, dim, 1)}
    buffers = {"F": scratch[0:8], "A": scratch[8:16]}
    sems = {"F": scratch[16:20], "A": scratch[20:24]}
    outs = {"F": sum_f_ref, "A": sum_a_ref}
    turns = {}
    for l in range(layers):
        for kind in kinds:
            made = kinds[kind].rounds(me, buffers[kind], sems[kind], l, outs[kind].at[l])
            for key, turn in made.items():
                turns[kind + str(l) + key] = turn

    def back_sems(l):
        return back_send.at[l], back_recv.at[l]

    def add_back(j, value):
        grad_ref[pl.ds(j * BLK, BLK), :] += value.astype(F32)

    def take_back(l):
        window.receive_back(back_ref.at[l], back_sems(l), add_back)
        window.send_back(win_low_ref, back_ref.at[l], back_sems(l), "wait_send")

    turns["R1"] = lambda: take_back(1)
    turns["R0"] = lambda: take_back(0)
    def early_sums():
        part_ref[0] = rows_ref[...]

    early = doubling_sum(me, early_sums, early_ref, part_ref, come_ref, few_send, few_recv)
    for i in range(6):
        turns["S" + str(i)] = early[i]
    turns["S6"] = lambda: [turn() for turn in early[6:]]

    def last_sums():
        late_part_ref[0] = jnp.zeros(late_part_ref.shape[1:], F32)
        for t in range(n):
            late_part_ref[0, t : t + 1, :] = rows_ref[12 + t : 13 + t, :]

    late = doubling_sum(me, last_sums, late_ref, late_part_ref, late_come_ref, late_send, late_recv)
    for i in range(6):
        turns["Q" + str(i)] = late[i]
    turns["Q6"] = lambda: [turn() for turn in late[6:]]

    @pl.when(step == 0)
    def _():
        load = pltpu.make_async_copy(grad_in_ref, grad_ref, grad_sem)
        load.start()
        met = meet(kinds["F"].peers(me) + me.beside())
        rows_ref[...] = jnp.zeros(rows_ref.shape, F32)
        load.wait()
        met()

    for i, names in enumerate(PLAN_BACK):
        if names:
            @pl.when(step == i)
            def _(names=names):
                for name in names:
                    turns[name]()

    def open_block(kind):
        scatter = kinds[kind]

        def core(l, block):
            return scatter.core(me, buffers[kind], sems[kind], l, block)

        @pl.when(r % 2 == 0)
        def _():
            core(layer, r // 2).wait_recv()

        @pl.when(r == 1)
        def _():
            core(layer, 1).wait_send()

        @pl.when(jnp.logical_and(r == 3, layer == 0))
        def _():
            core(1, 0).wait_send()

    def put(kind, lo, value):
        sums, stage = buffers[kind][:2]
        width = value.shape[1]
        value = value.reshape(n_dp, shard, width)

        @pl.when(r % 2 == 1)
        def _():
            stage[:, :, lo : lo + width] = value.astype(BF)

        @pl.when(r % 2 == 0)
        def _():
            block = kinds[kind].block(layer, r // 2)
            sums[block, :, :, lo : lo + width] = (sums[block, :, :, lo : lo + width].astype(F32) + value).astype(BF)

    def close_block(kind):
        scatter = kinds[kind]

        if scatter.sets == 1:
            @pl.when(jnp.logical_and(r == 3, layer == 0))
            def _():
                scatter.wait_credit(me, sems[kind])

        @pl.when(r % 2 == 1)
        def _():
            scatter.core(me, buffers[kind], sems[kind], layer, r // 2).start()

    @pl.when(phase == 0)
    def _():
        @pl.when(r == n - 1)
        def _():
            grad, unit = grad_ref[...], unit2_ref[0].astype(F32)
            dsecond = norm_back(grad, unit, rs2_ref[0], gain2_ref[line, :])
            rows_ref[pl.ds(at + 4, 1), :] = column_sum(grad * unit)
            rows_ref[pl.ds(at + 5, 1), :] = column_sum(grad)
            rows_ref[pl.ds(at + 3, 1), :] = column_sum(dsecond)
            acc_ref[...] = dsecond
            low_ref[...] = dsecond.astype(BF)
            low_t_ref[...] = dsecond.T.astype(BF)
            own_t_ref[...] = flip(mid_ref[0])

        @pl.when(r == 1)
        def _():
            pltpu.make_async_copy(win_ref.at[layer], win_low_ref, win_sem).start()

        dupper = dot(low_ref[...], down_ref[0, 0]) * slope_ref[0, 0].astype(F32)
        rows_ref[pl.ds(at + 8 + mine, 1), :] = column_sum(dupper)
        dupper_low = dupper.astype(BF)
        acc_ref[...] += dot_nt(dupper_low, up_ref[0, 0])
        open_block("F")
        put("F", 0, dot(own_t_ref[...], dupper_low))
        put("F", dim, dot(low_t_ref[...], act_ref[0, 0]))
        close_block("F")

        @pl.when(r == 0)
        def _():
            dmid, unit = acc_ref[...], unit1_ref[0].astype(F32)
            dfirst = norm_back(dmid, unit, rs1_ref[0], gain1_ref[line, :])
            rows_ref[pl.ds(at + 1, 1), :] = column_sum(dmid * unit)
            rows_ref[pl.ds(at + 2, 1), :] = column_sum(dmid)
            rows_ref[pl.ds(at, 1), :] = column_sum(dfirst)
            grad_ref[...] = dfirst
            low_ref[...] = dfirst.astype(BF)
            low_t_ref[...] = dfirst.T.astype(BF)

    @pl.when(phase == 1)
    def _():
        @pl.when(r == n - 1)
        def _():
            pltpu.make_async_copy(win_ref.at[layer], win_low_ref, win_sem).wait()
            own_t_ref[...] = flip(win_low_ref[own_rows, :])
            win_t_ref[...] = flip(win_low_ref[...])
            win_grad_ref[...] = jnp.zeros(win_grad_ref.shape, F32)

        dctx_ref[...] = dot(low_ref[...], g_ref[0, 0, :, 128:384]).astype(BF)
        dkv_ref[...] = jnp.zeros(dkv_ref.shape, F32)
        q_masks, c_masks = lane_masks(0, heads), lane_masks(1, heads)
        for j, (row, slot, part) in enumerate(window.blocks()):
            here = pl.ds(j * BLK, BLK)
            keys = pl.ds(pl.multiple_of(slot * PACK, PACK), PACK)
            q_stack = stack_heads(q_ref[0, 0, here, :], q_masks)
            d_stack = stack_heads(dctx_ref[here, :], c_masks)
            scores = dot_nt(kv_ref[0, 0, keys, 0:256], q_stack) * (HD**-0.5)
            scores = jnp.where(allowed_of(len_ref, row, part * BLK, 0, heads), scores, NEG)
            peak = jnp.max(scores, axis=0, keepdims=True)
            exps = jnp.exp(scores - peak)
            probs = exps * (1.0 / jnp.sum(exps, axis=0, keepdims=True))
            dprobs = dot_nt(kv_ref[0, 0, keys, 128:384], d_stack)
            weighted = probs * dprobs
            inner = jnp.sum(weighted, axis=0, keepdims=True)
            dscores = ((weighted - probs * inner) * (HD**-0.5)).astype(BF)
            dkv_ref[keys, 128:384] += dot(probs.astype(BF), d_stack)
            dkv_ref[keys, 0:256] += dot(dscores, q_stack)
            dq_ref[here, :] = pick_heads(dot_tn(dscores, kv_ref[0, 0, keys, 0:256]), q_masks, BLK)
        dq, dkv = dq_ref[...], dkv_ref[...]
        rows_ref[pl.ds(at + 12 + mine, 1), 0:256] = column_sum(dq)
        rows_ref[pl.ds(at + 12 + mine, 1), 256:640] = column_sum(dkv)
        dq_low, dkv_low = dq.astype(BF), dkv.astype(BF)
        grad_ref[...] += dot_nt(dq_low, g_ref[0, 0, :, 0:256])
        win_grad_ref[...] += dot_nt(dkv_low, g_ref[0, 0, :, 384:768])
        grad_q = dot(own_t_ref[...], dq_low)
        grad_o = dot(low_t_ref[...], ctx_ref[0, 0])
        open_block("A")
        put("A", 0, grad_q[:, 0:128])
        put("A", 128, grad_q[:, 128:256] + grad_o[:, 0:128])
        put("A", 256, grad_o[:, 128:256])
        put("A", 384, dot(win_t_ref[...], dkv_low))
        close_block("A")

        @pl.when(r == 0)
        def _():
            win_low_ref[...] = win_grad_ref[...].astype(BF)
            for l in range(layers):
                @pl.when(layer == l)
                def _(l=l):
                    window.send_back(win_low_ref, back_ref.at[l], back_sems(l))
            for j, place in enumerate(window.own_places()):
                grad_ref[pl.ds(j * BLK, BLK), :] += win_grad_ref[pl.ds(pl.multiple_of(place * BLK, BLK), BLK), :]

    @pl.when(step == pl.num_programs(0) - 1)
    def _():
        for name in LAST_BACK:
            turns[name]()
        for name in ("S6", "Q6", "F1E", "F0E", "A0E"):
            turns[name]()
        few_ref[...] = early_ref[...]
        few_ref[12 : 12 + n, :] = late_ref[0:n, :]
        store = pltpu.make_async_copy(grad_ref, grad_out_ref, grad_sem)
        store.start()
        for kind in kinds:
            kinds[kind].core(me, buffers[kind], sems[kind], 0, 0).wait_send()
        store.wait()


def backward(lens, grad, ga, gf, saved, gains, n_dp, n_tensor):
    q, kv, ctx, act, slope, mid, unit1, rs1, unit2, rs2, win = saved
    layers, n, (tokens, dim) = mid.shape[0], n_tensor, grad.shape
    shard = dim // n_dp
    blocks = 2 * (tokens // BLK)
    few = (16 * layers, dim)
    wide, narrow = Scatter(n_dp, shard, 2 * dim, layers), Scatter(n_dp, shard, dim, 1)

    def in_phase(phase, shape, *tail):
        held = 0 if phase == 0 else n - 1

        def at(s):
            r = jnp.where(s // n % 2 == phase, n - 1 - s % n, held)
            return (layers - 1 - s // (2 * n), r) + (tail if tail else (0, 0))
        return pl.BlockSpec((1, 1) + shape, at)

    def per_layer(shape):
        return pl.BlockSpec((1,) + shape, lambda s: (layers - 1 - s // (2 * n), 0, 0))

    doubling = doubling_scratch(few, n_dp, n_tensor) + doubling_scratch((8, dim), n_dp, n_tensor)
    doubling += [pltpu.VMEM(few, F32), pltpu.VMEM((8, dim), F32), pltpu.VMEM(few, F32)]
    return pl.pallas_call(
        functools.partial(backward_kernel, n_dp, n_tensor),
        grid=(2 * n * layers,),
        in_specs=[
            SMEM, HBM, in_phase(0, (dim, dim), 0, 0), in_phase(0, (dim, dim), 0, 1), in_phase(1, (dim, dim)),
            in_phase(0, (tokens, dim)), in_phase(0, (tokens, dim)),
            in_phase(1, (tokens, 256)), in_phase(1, (WIN, 384)), in_phase(1, (tokens, 256)),
            per_layer((tokens, dim)), per_layer((tokens, dim)), per_layer((tokens, 1)), per_layer((tokens, dim)), per_layer((tokens, 1)),
            HBM, whole(gains[0].shape), whole(gains[1].shape),
        ],
        out_specs=[HBM, HBM, HBM, whole(few)],
        out_shape=[sds((tokens, dim)), sds((layers, shard, 2 * dim)), sds((layers, shard, dim)), sds(few)],
        scratch_shapes=[
            pltpu.VMEM((tokens, dim), F32), pltpu.VMEM((tokens, dim), F32), pltpu.VMEM((tokens, dim), BF),
            pltpu.VMEM((dim, tokens), BF), pltpu.VMEM((dim, tokens), BF), pltpu.VMEM((dim, WIN), BF),
            pltpu.VMEM((tokens, 256), BF), pltpu.VMEM((tokens, 256), F32), pltpu.VMEM((WIN, 384), F32),
            pltpu.VMEM((WIN, dim), F32), pltpu.VMEM((WIN, dim), BF), pltpu.VMEM((layers, blocks, BLK, dim), BF),
        ]
        + doubling
        + [pltpu.SemaphoreType.DMA((layers, blocks)), pltpu.SemaphoreType.DMA((layers, blocks))] + [pltpu.SemaphoreType.DMA] * 2
        + wide.buffers() + narrow.buffers() + wide.sems(layers) + narrow.sems(layers),
        compiler_params=pltpu.CompilerParams(vmem_limit_bytes=67043328, collective_id=1, has_side_effects=True),
        name="backward",
    )(lens, grad, gf, gf, ga, act, slope, q, kv, ctx, mid, unit1, rs1, unit2, rs2, win, *gains)


def lay_out_kernel(
    n_dp, n_tensor, few_in, wf_in, wa_in, h_in, grad_in,
    h_out, grad_out, qkv_out, qv_out, ow_out, ob_out, gain1_out, shift1_out, up_out, ub_out, down_out, db_out, gain2_out, shift2_out,
    few_ref, wf_ref, wa_ref, sem,
):
    me = Place(n_dp, n_tensor)
    loads = [
        pltpu.make_async_copy(source, target, sem.at[i])
        for i, (source, target) in enumerate(
            ((wf_in, wf_ref), (wa_in, wa_ref), (few_in, few_ref), (h_in, h_out), (grad_in, grad_out))
        )
    ]
    for load in loads:
        load.start()
    for load in loads[:3]:
        load.wait()
    layers, units = qkv_out.shape[0], qkv_out.shape[3]
    dim, hidden = few_ref.shape[1], up_out.shape[2]
    wide, piece = ub_out.shape[1], qv_out.shape[2]
    def cut(row, start, size):
        return pltpu.roll(few_ref[pl.ds(row, 1), :], lax.rem(2 * dim - start, dim), 1)[:, 0:size]

    for l in range(layers):
        at = 16 * l
        for i, column in enumerate((0, 2, 3)):
            qkv_out[l, i] = wa_ref[l, :, column * units : (column + 1) * units]
        ow_out[l] = wa_ref[l, :, units : 2 * units].T
        up_out[l] = wf_ref[l, :, 0:hidden]
        down_out[l] = wf_ref[l, :, hidden : 2 * hidden]
        for k, out in enumerate((ob_out, gain1_out, shift1_out, db_out, gain2_out, shift2_out)):
            out[l : l + 1, :] = few_ref[at + k : at + k + 1, :]
        ub_out[l : l + 1, :] = cut(at + 8 + me.tensor, me.dp * wide, wide)
        qv_out[l, 0:1, :] = cut(at + 12 + me.tensor, Q_AT + me.dp * piece, piece)
        qv_out[l, 1:2, :] = cut(at + 12 + me.tensor, KV_AT + units + me.dp * piece, piece)
    for load in loads[3:]:
        load.wait()


def lay_out(few, wf, wa, h, grad, shapes, n_dp, n_tensor):
    return pl.pallas_call(
        functools.partial(lay_out_kernel, n_dp, n_tensor),
        in_specs=[HBM] * 5,
        out_specs=[VMEM] * len(shapes),
        out_shape=[sds(shape) for shape in shapes],
        scratch_shapes=[pltpu.VMEM(item.shape, F32) for item in (few, wf, wa)] + [pltpu.SemaphoreType.DMA((5,))],
        compiler_params=pltpu.CompilerParams(vmem_limit_bytes=67043328),
        name="lay_out",
    )(few, wf, wa, h, grad)


def body(n_dp, n_tensor, block_input, passage_lengths, qkv_weight, qv_bias, out_weight, out_bias, first_gain,
         first_shift, up_weight, up_bias, down_weight, down_bias, second_gain, second_shift, output_grad):
    layers = qkv_weight.shape[0]
    tokens, dim = block_input.shape
    rows = passage_lengths.shape[0]
    shard = qkv_weight.shape[2]
    lens = passage_lengths

    vecs = [out_bias, first_gain, first_shift, down_bias, second_gain, second_shift]
    q, kv, ctx, act, slope, mid, unit1, rs1, unit2, rs2, block_output, win, ga, gf, _ = forward(
        lens, qkv_weight, out_weight, up_weight, down_weight.transpose(0, 2, 1), qv_bias, up_bias, block_input, vecs, n_dp, n_tensor
    )
    ga, gf = (g.reshape(layers, n_tensor, n_dp * shard, g.shape[-1]) for g in (ga, gf))

    saved = (q, kv, ctx, act, slope, mid, unit1, rs1, unit2, rs2, win)
    grad, wf, wa, totals = backward(lens, output_grad, ga, gf, saved, [first_gain, second_gain], n_dp, n_tensor)

    shapes = [(tokens, dim)] * 2 + [
        item.shape
        for item in (qkv_weight, qv_bias, out_weight, out_bias, first_gain, first_shift,
                     up_weight, up_bias, down_weight, down_bias, second_gain, second_shift)
    ]
    down_at = 10
    layer, units, columns = shapes[down_at]
    shapes[down_at] = (layer, columns, units)
    results = list(lay_out(totals, wf, wa, block_output, grad, shapes, n_dp, n_tensor))
    results[down_at] = results[down_at].transpose(0, 2, 1)
    return tuple(results)


def solution(mesh):
    n_dp, n_tensor = mesh.shape["dp"], mesh.shape["tensor"]
    tokens = P(("dp", "tensor"), None)
    in_specs = (
        tokens, P("dp", None), P(None, None, "dp", "tensor"), P(None, None, ("tensor", "dp")), P(None, "tensor", "dp"),
        P(), P(), P(), P(None, "dp", "tensor"), P(None, ("tensor", "dp")), P(None, "tensor", "dp"), P(), P(), P(), tokens,
    )
    out_specs = (
        tokens, tokens, P(None, None, "dp", "tensor"), P(None, None, ("tensor", "dp")), P(None, "tensor", "dp"),
        P(), P(), P(), P(None, "dp", "tensor"), P(None, ("tensor", "dp")), P(None, "tensor", "dp"), P(), P(), P(),
    )
    return jax.shard_map(
        functools.partial(body, n_dp, n_tensor), mesh=mesh, in_specs=in_specs, out_specs=out_specs, check_vma=False
    )
```
